32 devices in a mesh: sta: 8 (over y, x, core), hour: 4 (over z).
Axes of the slice: x: 2, y: 2, z: 4, core: 2. Of those that a mesh axis runs over, the one named last changes fastest.
Arguments:
- spectra: bfloat16 [128, 4, 30, 2, 1024], P('sta', 'hour'), may hold values from -1000 to 1000
- band_weight: float32 [1024], replicated, may hold values from 0.5 to 4
- station_order: int32 [8, 16], P('sta'), may hold values from 0 to 15, each once within a row
- pair_blocks: int32 [16, 2], P('sta'), may hold values from 0 to 7, as said below
Outputs:
- cross: float32 [16, 16, 16, 2, 1024], P('sta', None, None, None, 'hour')
The draws below stay inside these ranges and needn't reach their ends.
Inputs may be any that keep to these rules, and one draw needn't show every extreme that they name: `pair_blocks`: the first block of each pair block belongs to the station group that owns the pair block (pair p to group p // 2); the second belongs to that group or to a group next to it, and every group asks at least once for a block of each group next to it.
All inputs are finite; a program needn't handle non-finite values.
Results may differ from the reference program's by a relative error of at most 0.0041.
Values may be sent and summed in bfloat16 or wider, within the bound.
No kernel may reach another device: no remote copies, remote signals or barrier semaphores. Data moves between devices by JAX's collectives and lax.ppermute only.
A program may use at most 192 MiB of HBM per device.

```python
import math
import jax
import jax.numpy as jnp
from jax import lax

F = 1024
WINDOWS = 30
STATION_BLOCK = 16
BLK_DEV = 1
STA_DEV = 16
PB_DEV = 2
GROUPS = 8
STATIONS = 128
NBLK = 8
PAIRS = 16
HOURS = 4


def draw_spectra(key, part):
    keys = jax.random.split(key, 4)
    shape = (STATIONS, HOURS, WINDOWS, 2, F)
    base = jnp.clip(jax.random.normal(keys[0], shape, jnp.float32), -6.0, 6.0)
    station_scale = jnp.exp(jax.random.uniform(keys[1], (STATIONS, 1, 1, 1, 1), jnp.float32, 0.0, 2.3))
    bin_scale = jnp.exp(jax.random.uniform(keys[2], (1, 1, 1, 2, F), jnp.float32, 0.0, 2.3))
    window_scale = jnp.exp(jax.random.uniform(keys[3], (STATIONS, HOURS, WINDOWS, 1, 1), jnp.float32, -0.7, 0.7))
    values = base * station_scale * bin_scale * window_scale
    return jnp.clip(values, -1000.0, 1000.0).astype(jnp.bfloat16)


def draw_pair_blocks(key, part):
    keys = jax.random.split(key, 4)
    owner = jnp.arange(PAIRS, dtype=jnp.int32) // PB_DEV
    local_first = jax.random.randint(keys[0], (PAIRS,), 0, BLK_DEV, dtype=jnp.int32)
    first = owner * BLK_DEV + local_first

    def slot_places(group):
        return jax.random.permutation(jax.random.fold_in(keys[1], group), PB_DEV).astype(jnp.int32)
    places = jax.vmap(slot_places)(jnp.arange(GROUPS, dtype=jnp.int32)).reshape(-1)
    random_step = jax.random.randint(keys[2], (PAIRS,), -1, 2, dtype=jnp.int32)
    step = jnp.where(places == 0, -1, jnp.where(places == 1, 1, random_step))
    neighbour = owner + step
    neighbour = jnp.where(neighbour < 0, 1, jnp.where(neighbour >= GROUPS, GROUPS - 2, neighbour))
    local_second = jax.random.randint(keys[3], (PAIRS,), 0, BLK_DEV, dtype=jnp.int32)
    second = neighbour * BLK_DEV + local_second
    return jnp.stack([first, second], axis=1).astype(jnp.int32)


def setup_inputs(seed: int = 0) -> dict:
    arg_keys = jax.random.split(jax.random.key(seed), 5)
    return {
        "spectra": draw_spectra(jax.random.fold_in(arg_keys[4], 71), 0),
        "band_weight": jnp.clip(jnp.exp(jax.random.uniform(arg_keys[1], (F,), jnp.float32, math.log(0.5), math.log(4.0))), 0.5, 4.0),
        "station_order": jax.vmap(lambda own: jax.random.permutation(own, STA_DEV))(jax.random.split(arg_keys[2], GROUPS)).reshape((GROUPS, STA_DEV)).astype(jnp.int32),
        "pair_blocks": draw_pair_blocks(jax.random.fold_in(arg_keys[4], 71), 0),
    }


def reference(spectra, band_weight, station_order, pair_blocks):
    values = spectra.astype(jnp.float32)
    energy = lax.optimization_barrier(jnp.mean(values * values, axis=(3, 4), keepdims=True))
    white = (values * lax.rsqrt(energy + 1e-06) * band_weight).astype(jnp.bfloat16)
    index = (jnp.arange(GROUPS, dtype=jnp.int32)[:, None] * STA_DEV + station_order).reshape(-1)
    blocks = white[index].reshape(NBLK, STATION_BLOCK, HOURS, WINDOWS, 2, F)

    def one_pair(pair):
        left = blocks[pair[0]].astype(jnp.float32)
        right = blocks[pair[1]].astype(jnp.float32)
        hp = lax.Precision.HIGHEST
        real_part = jnp.einsum('shwf,thwf->stf', left[:, :, :, 0], right[:, :, :, 0], precision=hp) + jnp.einsum('shwf,thwf->stf', left[:, :, :, 1], right[:, :, :, 1], precision=hp)
        imag_part = jnp.einsum('shwf,thwf->stf', left[:, :, :, 0], right[:, :, :, 1], precision=hp) - jnp.einsum('shwf,thwf->stf', left[:, :, :, 1], right[:, :, :, 0], precision=hp)
        return jnp.stack([real_part, imag_part], axis=2) / (HOURS * WINDOWS)
    return lax.map(one_pair, pair_blocks)
```

```python
import jax
import jax.numpy as jnp
from jax import lax
from jax.experimental import pallas as pl
from jax.experimental.pallas import tpu as pltpu
from jax.sharding import PartitionSpec as P

LANES = 128
EPSILON = 1e-06
EDGES = 2
GROUPS = ((2,), (1,), (3,), (0,))


def whiten(spectra, band_weight, station_order):
    stations, windows, rows, _ = spectra.shape
    tiles = rows // 2
    step = 6
    hours = tiles // EDGES
    bins = tiles * LANES
    height = 2 * stations

    def body(order_ref, x_ref, band_ref, *refs):
        outs, (band, rowed) = refs[:-2], refs[-2:]

        @pl.when(pl.program_id(0) == 0)
        def _():
            for part in range(2):
                band[pl.ds(part, tiles, stride=2), :] = band_ref[...]

        weight = band[...]
        for w in range(step):
            for s in range(stations):
                x = x_ref[order_ref[0, s], w].astype(jnp.float32)
                energy = jnp.sum(x * x, axis=(0, 1), keepdims=True) / (2 * bins)
                white = x * lax.rsqrt(energy + EPSILON) * weight
                white = white.astype(jnp.bfloat16).astype(jnp.float32)
                rowed[pl.ds(w * rows * stations + s, rows, stride=stations), :] = white
        here = lax.axis_index("hour")
        k = 0
        for edge in range(EDGES):
            for group in GROUPS:
                for i, d in enumerate(group):
                    owner = lax.rem(here + d, hours)
                    for w in range(step):
                        start = (w * tiles + owner * EDGES + edge) * height
                        tile = rowed[pl.ds(pl.multiple_of(start, height), height), :]
                        outs[k][i, w] = tile.astype(jnp.bfloat16)
                k += 1

    shapes = [
        jax.ShapeDtypeStruct((len(group), windows, height, LANES), jnp.bfloat16)
        for _ in range(EDGES)
        for group in GROUPS
    ]
    outs = pl.pallas_call(
        body,
        grid=(windows // step,),
        in_specs=[
            pl.BlockSpec(memory_space=pltpu.SMEM),
            pl.BlockSpec((stations, step, rows, LANES), lambda i: (0, i, 0, 0)),
            pl.BlockSpec((tiles, LANES), lambda i: (0, 0)),
        ],
        out_specs=[
            pl.BlockSpec((len(group), step, height, LANES), lambda i: (0, i, 0, 0))
            for _ in range(EDGES)
            for group in GROUPS
        ],
        out_shape=shapes,
        scratch_shapes=[
            pltpu.VMEM((rows, LANES), jnp.float32),
            pltpu.VMEM((step * rows * stations, LANES), jnp.float32),
        ],
        name="whiten",
    )(station_order, spectra, band_weight)
    count = len(GROUPS)
    return outs[:count], outs[count:]


def unit(own_ref, other_ref, out_ref, wide):
    windows, height, _ = own_ref.shape
    stations = height // 2
    block = 8
    wide[...] = own_ref[...].astype(jnp.float32).reshape(windows * height, LANES)
    for first in range(0, stations, block):

        def body(w, sums):
            other = other_ref[w].astype(jnp.float32)
            re, im = other[:stations], other[stations:]
            new = []
            for i in range(block):
                row = w * height + first + i
                a_re = jnp.broadcast_to(wide[pl.ds(row, 1), :], re.shape)
                a_im = jnp.broadcast_to(wide[pl.ds(row + stations, 1), :], re.shape)
                new.append(sums[2 * i] + a_re * re + a_im * im)
                new.append(sums[2 * i + 1] + a_re * im - a_im * re)
            return tuple(new)

        zero = jnp.zeros((stations, LANES), jnp.float32)
        sums = lax.fori_loop(0, windows, body, (zero,) * (2 * block))
        for i in range(block):
            out_ref[first + i, :stations] = sums[2 * i].astype(out_ref.dtype)
            out_ref[first + i, stations:] = sums[2 * i + 1].astype(out_ref.dtype)


def products(pair_blocks, own, other, dtype):
    pieces, windows, height, _ = own[0].shape
    stations = height // 2

    def body(pairs_ref, *refs):
        own_refs, other_refs, outs = refs[:EDGES], refs[EDGES : 2 * EDGES], refs[2 * EDGES : -2]
        wide, twin = refs[-2:]
        me, count = lax.axis_index("sta"), lax.axis_size("sta")
        asked = pairs_ref[0, 1] == me
        for p in range(1, pairs_ref.shape[0]):
            asked = jnp.logical_or(asked, pairs_ref[p, 1] == me)
        for i in range(pieces):
            for edge in range(EDGES):
                alone = jnp.logical_and(asked, me == (count - 1 if edge else 0))
                out = outs[i].at[edge]

                @pl.when(jnp.logical_not(alone))
                def _(i=i, edge=edge, out=out):
                    unit(own_refs[edge].at[i], other_refs[edge].at[i], out, wide)

                @pl.when(alone)
                def _(i=i, edge=edge, out=out):
                    unit(own_refs[0].at[i], own_refs[0].at[i], twin.at[0], wide)
                    unit(own_refs[1].at[i], own_refs[1].at[i], twin.at[1], wide)
                    column = lax.broadcasted_iota(jnp.int32, (stations, LANES), 0)

                    @pl.loop(0, stations)
                    def _(a):
                        one, two = twin[0, a], twin[1, a]
                        re = jnp.where(column >= a, one[:stations], two[:stations])
                        im = jnp.where(column >= a, one[stations:], two[stations:])
                        im = jnp.where(column == a, two[:stations], im)
                        out[a, :stations] = re.astype(dtype)
                        out[a, stations:] = im.astype(dtype)

    whole = pl.BlockSpec((pieces, windows, height, LANES), lambda: (0, 0, 0, 0))
    shape = (EDGES, stations, height, LANES)
    flops = pieces * EDGES * stations * stations * LANES * windows * 8
    return pl.pallas_call(
        body,
        in_specs=[pl.BlockSpec(memory_space=pltpu.SMEM)] + [whole] * (2 * EDGES),
        out_specs=[pl.BlockSpec(shape, lambda: (0, 0, 0, 0))] * pieces,
        out_shape=[jax.ShapeDtypeStruct(shape, dtype)] * pieces,
        scratch_shapes=[
            pltpu.VMEM((windows * height, LANES), jnp.float32),
            pltpu.VMEM((2, stations, height, LANES), jnp.float32),
        ],
        cost_estimate=pl.CostEstimate(flops=flops, bytes_accessed=1 << 20, transcendentals=0),
        name="products",
    )(pair_blocks, *own, *other)


def add_hours(parts, scale):
    shape = parts[0].shape
    edges, stations, height, _ = shape

    def body(*refs):
        parts_refs, (own_out, turned_0, turned_1), buf = refs[: len(parts)], refs[len(parts) : -1], refs[-1]
        for edge in range(edges):
            for a in range(stations):
                total = parts_refs[0][edge, a].astype(jnp.float32)
                for ref in parts_refs[1:]:
                    total = total + ref[edge, a].astype(jnp.float32)
                total = total * scale
                own_out[edge, a] = total
                for part in range(2):
                    rows = total[part * stations : (part + 1) * stations]
                    if part:
                        rows = -rows
                    buf[edge, pl.ds(part * stations + a, stations, stride=height), :] = rows
        turned_0[...] = buf[0].reshape(stations, height, LANES).astype(turned_0.dtype)
        turned_1[...] = buf[1].reshape(stations, height, LANES).astype(turned_1.dtype)

    return pl.pallas_call(
        body,
        out_shape=[
            jax.ShapeDtypeStruct(shape, jnp.float32),
            jax.ShapeDtypeStruct(shape[1:], jnp.float32),
            jax.ShapeDtypeStruct(shape[1:], jnp.float32),
        ],
        scratch_shapes=[pltpu.VMEM((edges, stations * height, LANES), jnp.float32)],
        name="add_hours",
    )(*parts)


def assemble(pair_blocks, own, turned, other):
    edges, stations, height, _ = own.shape
    pairs = pair_blocks.shape[0]

    def body(pairs_ref, own_ref, turned_0, turned_1, other_0, other_1, out_ref):
        me, count = lax.axis_index("sta"), lax.axis_size("sta")
        turned_refs, other_refs = (turned_0, turned_1), (other_0, other_1)

        def put(p, a, tile, re, im):
            lanes = pl.ds(tile * LANES, LANES)
            out_ref[p, a, :, 0, lanes] = re
            out_ref[p, a, :, 1, lanes] = im

        for p in range(pairs):
            step = pairs_ref[p, 1] - me

            for edge in range(edges):

                @pl.when(step == 2 * edge - 1)
                def _(p=p, edge=edge):
                    for a in range(stations):
                        mine, theirs = own_ref[edge, a], other_refs[edge][a]
                        put(p, a, edge, mine[:stations], mine[stations:])
                        put(p, a, 1 - edge, theirs[:stations], theirs[stations:])

                @pl.when(jnp.logical_and(step == 0, me == (count - 1 if edge else 0)))
                def _(p=p, edge=edge):
                    column = lax.broadcasted_iota(jnp.int32, (stations, LANES), 0)
                    for a in range(stations):
                        mine, turned = own_ref[edge, a], turned_refs[edge][a]
                        m_re, m_im = mine[:stations], mine[stations:]
                        t_re, t_im = turned[:stations], turned[stations:]
                        zero = jnp.zeros_like(m_im)
                        put(
                            p, a, 0, jnp.where(column >= a, m_re, t_re),
                            jnp.where(column == a, zero, jnp.where(column > a, m_im, t_im)),
                        )
                        put(
                            p, a, 1,
                            jnp.where(column == a, m_im, jnp.where(column < a, m_re, t_re)),
                            jnp.where(column == a, zero, jnp.where(column < a, m_im, t_im)),
                        )

    vmem = pl.BlockSpec(memory_space=pltpu.VMEM)
    return pl.pallas_call(
        body,
        in_specs=[pl.BlockSpec(memory_space=pltpu.SMEM)] + [vmem] * 5,
        out_specs=vmem,
        out_shape=jax.ShapeDtypeStruct((pairs, stations, stations, 2, edges * LANES), jnp.float32),
        name="assemble",
    )(pair_blocks, own, *turned, *other)


def per_device(spectra, band_weight, station_order, pair_blocks):
    stations, _, windows, _, bins = spectra.shape
    tiles = bins // LANES
    count, hours = lax.axis_size("sta"), lax.axis_size("hour")
    rows = spectra.reshape(stations, windows, 2, tiles, LANES)
    rows = rows.transpose(0, 1, 3, 2, 4).reshape(stations, windows, 2 * tiles, LANES)
    own = whiten(rows, band_weight.reshape(tiles, LANES), station_order)

    up = [(i, i + 1) for i in range(count - 1)]
    down = [(j, i) for i, j in up]
    moved = [
        (lax.ppermute(own[0][k], "sta", up), lax.ppermute(own[1][k], "sta", down))
        for k in range(len(GROUPS))
    ]
    parts = []
    for k, group in enumerate(GROUPS):
        made = products(pair_blocks, (own[0][k], own[1][k]), moved[k], jnp.bfloat16)
        for d, piece in zip(group, made):
            if d:
                piece = lax.ppermute(piece, "hour", [(h, (h + d) % hours) for h in range(hours)])
            parts.append(piece)
    mine, turned_0, turned_1 = add_hours(parts, 1.0 / (hours * windows))
    other_0 = lax.ppermute(turned_1, "sta", up)
    other_1 = lax.ppermute(turned_0, "sta", down)
    return assemble(pair_blocks, mine, (turned_0, turned_1), (other_0, other_1))


def solution(mesh):
    return jax.shard_map(
        per_device,
        mesh=mesh,
        in_specs=(P("sta", "hour", None, None, None), P(), P("sta", None), P("sta", None)),
        out_specs=P("sta", None, None, None, "hour"),
        check_vma=False,
    )
```

```python
import jax
import jax.numpy as jnp
from jax import lax
from jax.experimental import pallas as pl
from jax.experimental.pallas import tpu as pltpu
from jax.sharding import PartitionSpec as P

LANES = 128
EPSILON = 1e-06
BLOCK = 8
WIDE = jnp.float32
SMEM = pl.BlockSpec(memory_space=pltpu.SMEM)
VMEM = pl.BlockSpec(memory_space=pltpu.VMEM)


def limits(mib):
    return pltpu.CompilerParams(vmem_limit_bytes=mib << 20)


def asks_itself(pairs_ref, me):
    asked = pairs_ref[0, 1] == me
    for p in range(1, pairs_ref.shape[0]):
        asked = jnp.logical_or(asked, pairs_ref[p, 1] == me)
    return asked


def whiten(spectra, band_weight, station_order, pair_blocks, hours):
    stations, windows, rows, _ = spectra.shape
    tiles = rows // 2
    mine = tiles // hours
    step = windows // 5
    chunks = windows // step
    height = 2 * stations

    def body(order_ref, pairs_ref, band_ref, x_hbm, *refs):
        outs, (band, rowed, x_ref, sems) = refs[:hours], refs[hours:]

        def fetch(c):
            part = pl.ds(c * step, step)
            return pltpu.make_async_copy(x_hbm.at[:, part], x_ref.at[:, part], sems.at[c])

        for c in range(chunks):
            fetch(c).start()
        for part in range(2):
            band[pl.ds(part, tiles, stride=2), :] = band_ref[...]
        weight = band[...]
        here = lax.axis_index("hour")
        asked = asks_itself(pairs_ref, lax.axis_index("sta"))
        flag = jnp.where(asked, 1.0, 0.0)
        for out in outs:
            out[mine * windows] = jnp.full((height, LANES), flag, WIDE).astype(jnp.bfloat16)

        @pl.loop(0, chunks)
        def _(c):
            fetch(c).wait()
            for w in range(step):
                for first in range(0, stations, BLOCK):
                    xs, squares = [], []
                    for k in range(BLOCK):
                        x = x_ref[order_ref[0, first + k], c * step + w].astype(WIDE)
                        xs.append(x)
                        squares.append(jnp.sum(x * x, axis=0, keepdims=True))
                    energy = jnp.sum(jnp.concatenate(squares, axis=0), axis=1, keepdims=True)
                    scale = lax.rsqrt(energy / (rows * LANES) + EPSILON)
                    scale = jnp.broadcast_to(scale, (BLOCK, LANES))
                    for k, x in enumerate(xs):
                        factor = jnp.broadcast_to(scale[k : k + 1], (rows, LANES))
                        place = pl.ds(w * rows * stations + first + k, rows, stride=stations)
                        rowed[place, :] = x * factor * weight
            for d in range(hours):
                owner = lax.rem(here + d, hours)
                for tile in range(mine):
                    for w in range(step):
                        start = (w * tiles + owner * mine + tile) * height
                        white = rowed[pl.ds(pl.multiple_of(start, height), height), :]
                        outs[d][tile * windows + c * step + w] = white.astype(jnp.bfloat16)

    shape = (mine * windows + 1, height, LANES)
    return pl.pallas_call(
        body,
        in_specs=[SMEM, SMEM, VMEM, pl.BlockSpec(memory_space=pltpu.HBM)],
        out_specs=[VMEM] * hours,
        out_shape=[jax.ShapeDtypeStruct(shape, jnp.bfloat16)] * hours,
        scratch_shapes=[
            pltpu.VMEM((rows, LANES), WIDE),
            pltpu.VMEM((step * rows * stations, LANES), WIDE),
            pltpu.VMEM(spectra.shape, jnp.bfloat16),
            pltpu.SemaphoreType.DMA((chunks,)),
        ],
        compiler_params=limits(8),
        name="whiten",
    )(station_order, pair_blocks, band_weight, spectra)


def unit(first_row, windows, own_ref, other_ref, out_ref, wide):
    stations = own_ref.shape[1] // 2
    rows = pl.ds(first_row, windows)
    wide[...] = own_ref[rows].astype(WIDE)
    for first in range(0, stations, BLOCK):

        def body(w, sums):
            other = other_ref[first_row + w].astype(WIDE)
            re, im = other[:stations], other[stations:]
            new = []
            for k in range(BLOCK):
                a = first + k
                a_re = jnp.broadcast_to(wide[w, a : a + 1, :], re.shape)
                a_im = jnp.broadcast_to(wide[w, stations + a : stations + a + 1, :], re.shape)
                new.append(sums[2 * k] + (a_re * re + a_im * im))
                new.append(sums[2 * k + 1] + (a_re * im - a_im * re))
            return tuple(new)

        zero = jnp.zeros((stations, LANES), WIDE)
        sums = lax.fori_loop(0, windows, body, (zero,) * (2 * BLOCK), unroll=6)
        for k in range(BLOCK):
            out_ref[first + k, :stations] = sums[2 * k].astype(out_ref.dtype)
            out_ref[first + k, stations:] = sums[2 * k + 1].astype(out_ref.dtype)


def products(pair_blocks, own, other, windows, dtype):
    entries, height, _ = own.shape
    tiles, stations = (entries - 1) // windows, height // 2

    def body(pairs_ref, own_ref, other_ref, out_ref, wide, twin):
        me = lax.axis_index("sta")
        last = me == lax.axis_size("sta") - 1
        flags = other_ref[entries - 1].astype(WIDE)
        asked = jnp.logical_or(asks_itself(pairs_ref, me), jnp.max(flags) > 0.5)
        alone = jnp.logical_and(last, asked)

        @pl.when(jnp.logical_not(alone))
        def _():
            for tile in range(tiles):
                unit(tile * windows, windows, own_ref, other_ref, out_ref.at[tile], wide)

        @pl.when(alone)
        def _():
            column = lax.broadcasted_iota(jnp.int32, (stations, LANES), 0)
            for tile in range(tiles):
                for k, ref in enumerate((own_ref, other_ref)):
                    unit(tile * windows, windows, ref, ref, twin.at[k], wide)

                @pl.loop(0, stations)
                def _(a, tile=tile):
                    one, two = twin[0, a], twin[1, a]
                    re = jnp.where(column >= a, one[:stations], two[:stations])
                    im = jnp.where(column >= a, one[stations:], two[stations:])
                    im = jnp.where(column == a, two[:stations], im)
                    out_ref[tile, a, :stations] = re.astype(dtype)
                    out_ref[tile, a, stations:] = im.astype(dtype)

    flops = tiles * stations * stations * LANES * windows * 8
    return pl.pallas_call(
        body,
        in_specs=[SMEM, VMEM, VMEM],
        out_specs=VMEM,
        out_shape=jax.ShapeDtypeStruct((tiles, stations, height, LANES), dtype),
        scratch_shapes=[
            pltpu.VMEM((windows, height, LANES), WIDE),
            pltpu.VMEM((2, stations, height, LANES), WIDE),
        ],
        compiler_params=limits(4),
        cost_estimate=pl.CostEstimate(flops=flops, bytes_accessed=1 << 20, transcendentals=0),
        name="products",
    )(pair_blocks, own, other)


def turn(a, value, buf_ref):
    height = value.shape[0]
    stations = height // 2
    for part in range(2):
        rows = value[part * stations : (part + 1) * stations]
        buf_ref[pl.ds(part * stations + a, stations, stride=height), :] = -rows if part else rows


def add_hours(parts, scale):
    shape = parts[0].shape
    tiles, stations, height, _ = shape

    def body(*refs):
        part_refs, (mine_ref, turned_ref, buf) = refs[: len(parts)], refs[len(parts) :]
        for tile in range(tiles):
            for a in range(stations):
                total = part_refs[0][tile, a].astype(WIDE)
                for ref in part_refs[1:]:
                    total = total + ref[tile, a].astype(WIDE)
                total = total * scale
                mine_ref[tile, a] = total
                turn(a, total, buf.at[tile])
            for c in range(stations):
                rows = buf[tile, pl.ds(c * height, height), :]
                turned_ref[tile, c] = rows.astype(turned_ref.dtype)

    return pl.pallas_call(
        body,
        in_specs=[VMEM] * len(parts),
        out_specs=[VMEM] * 2,
        out_shape=[jax.ShapeDtypeStruct(shape, WIDE), jax.ShapeDtypeStruct(shape, jnp.bfloat16)],
        scratch_shapes=[pltpu.VMEM((tiles, stations * height, LANES), WIDE)],
        compiler_params=limits(4),
        name="add_hours",
    )(*parts)


def assemble(pair_blocks, mine, turned, other):
    tiles, stations, height, _ = mine.shape
    pairs = pair_blocks.shape[0]

    def body(pairs_ref, mine_ref, turned_ref, other_ref, out_ref, buf):
        me, count = lax.axis_index("sta"), lax.axis_size("sta")
        column = lax.broadcasted_iota(jnp.int32, (stations, LANES), 0)

        def put(p, a, tile, value):
            for part in range(2):
                rows = value[part * stations : (part + 1) * stations]
                out_ref[p, a, pl.ds(tile * 2 + part, stations, stride=2 * tiles), :] = rows

        def hermitian(p, a, tile, above, below, middle):
            re = jnp.where(column > a, above[:stations], below[:stations])
            im = jnp.where(column > a, above[stations:], below[stations:])
            re = jnp.where(column == a, middle, re)
            im = jnp.where(column == a, jnp.zeros_like(im), im)
            put(p, a, tile, jnp.concatenate([re, im], axis=0))

        for p in range(pairs):
            step = pairs_ref[p, 1] - me

            @pl.when(step == 1)
            def _(p=p):
                for tile in range(tiles):
                    for a in range(stations):
                        put(p, a, tile, mine_ref[tile, a])

            @pl.when(step == -1)
            def _(p=p):
                for tile in range(tiles):
                    for a in range(stations):
                        put(p, a, tile, other_ref[tile, a].astype(WIDE))

            @pl.when(jnp.logical_and(step == 0, me == count - 1))
            def _(p=p):
                for tile in range(tiles):
                    for a in range(stations):
                        own = mine_ref[tile, a]
                        back = turned_ref[tile, a].astype(WIDE)
                        hermitian(p, a, tile, own, back, own[:stations])

            @pl.when(jnp.logical_and(step == 0, me == 0))
            def _(p=p):
                for tile in range(tiles):
                    for a in range(stations):
                        turn(a, other_ref[tile, a].astype(WIDE), buf.at[tile])
                    for a in range(stations):
                        theirs = other_ref[tile, a].astype(WIDE)
                        back = buf[tile, pl.ds(a * height, height), :]
                        hermitian(p, a, tile, theirs, back, -theirs[stations:])

    rows = stations * tiles * 2
    return pl.pallas_call(
        body,
        in_specs=[SMEM, VMEM, VMEM, VMEM],
        out_specs=VMEM,
        out_shape=jax.ShapeDtypeStruct((pairs, stations, rows, LANES), WIDE),
        scratch_shapes=[pltpu.VMEM((tiles, stations * height, LANES), WIDE)],
        compiler_params=limits(4),
        name="assemble",
    )(pair_blocks, mine, turned, other)


def per_device(spectra, band_weight, station_order, pair_blocks):
    stations, _, windows, _, bins = spectra.shape
    tiles, pairs = bins // LANES, pair_blocks.shape[0]
    count, hours = lax.axis_size("sta"), lax.axis_size("hour")
    rows = spectra.reshape(stations, windows, 2, tiles, LANES)
    rows = rows.transpose(0, 1, 3, 2, 4).reshape(stations, windows, 2 * tiles, LANES)
    own = whiten(rows, band_weight.reshape(tiles, LANES), station_order, pair_blocks, hours)

    down = [((i + 1) % count, i) for i in range(count)]
    up = [(j, i) for i, j in down]
    order = [2, 1, 3, 0]
    other = {d: lax.ppermute(own[d], "sta", down) for d in order}
    parts = []
    for d in order:
        piece = products(pair_blocks, own[d], other[d], windows, jnp.bfloat16 if d else WIDE)
        if d:
            piece = lax.ppermute(piece, "hour", [(h, (h + d) % hours) for h in range(hours)])
        parts.append(piece)
    mine, turned = add_hours(parts, 1.0 / (hours * windows))
    theirs = lax.ppermute(turned, "sta", up)
    cross = assemble(pair_blocks, mine, turned, theirs)
    cross = cross.reshape(pairs, stations, stations, tiles // hours, 2, LANES)
    return cross.transpose(0, 1, 2, 4, 3, 5).reshape(pairs, stations, stations, 2, bins // hours)


def solution(mesh):
    return jax.shard_map(
        per_device,
        mesh=mesh,
        in_specs=(P("sta", "hour", None, None, None), P(), P("sta", None), P("sta", None)),
        out_specs=P("sta", None, None, None, "hour"),
        check_vma=False,
    )
```

```python
import jax
import jax.numpy as jnp
from jax import lax
from jax.experimental import pallas as pl
from jax.experimental.pallas import tpu as pltpu
from jax.sharding import PartitionSpec as P

LANES = 128
EPSILON = 1e-06
BLOCK = 8
PIECES = (((0, 2), (1, 2)), ((0, 1), (1, 1)), ((0, 3), (1, 3)), ((0, 0), (1, 0)))
WIDE = jnp.float32
SMEM = pl.BlockSpec(memory_space=pltpu.SMEM)
VMEM = pl.BlockSpec(memory_space=pltpu.VMEM)


def limits(mib):
    return pltpu.CompilerParams(vmem_limit_bytes=mib << 20)


def asks_itself(pairs_ref, me):
    asked = pairs_ref[0, 1] == me
    for p in range(1, pairs_ref.shape[0]):
        asked = jnp.logical_or(asked, pairs_ref[p, 1] == me)
    return asked


def whiten(spectra, band_weight, station_order, pair_blocks, hours):
    stations, windows, rows, _ = spectra.shape
    tiles = rows // 2
    mine = tiles // hours
    chunks = 5
    step = windows // chunks
    height = 2 * stations

    def body(order_hbm, pairs_hbm, band_hbm, x_hbm, *refs):
        outs = refs[: len(PIECES)]
        order_ref, pairs_ref, band_ref, band, rowed, x_ref, sems, small = refs[len(PIECES) :]

        def fetch(c):
            part = pl.ds(c * step, step)
            return pltpu.make_async_copy(x_hbm.at[:, part], x_ref.at[:, part], sems.at[c])

        fetch(0).start()
        copies = [
            pltpu.make_async_copy(order_hbm, order_ref, small.at[0]),
            pltpu.make_async_copy(pairs_hbm, pairs_ref, small.at[1]),
            pltpu.make_async_copy(band_hbm, band_ref, small.at[2]),
        ]
        for copy in copies:
            copy.start()
        for c in range(1, chunks):
            fetch(c).start()
        for copy in copies:
            copy.wait()
        for part in range(2):
            band[pl.ds(part, tiles, stride=2), :] = band_ref[...]
        weight = band[...]
        here = lax.axis_index("hour")
        asked = asks_itself(pairs_ref, lax.axis_index("sta"))
        flag = jnp.where(asked, 1.0, 0.0)
        for piece, out in zip(PIECES, outs):
            out[len(piece) * windows] = jnp.full((height, LANES), flag, WIDE).astype(jnp.bfloat16)

        @pl.loop(0, chunks)
        def _(c):
            fetch(c).wait()
            for w in range(step):
                for first in range(0, stations, BLOCK):
                    xs, squares = [], []
                    for k in range(BLOCK):
                        x = x_ref[order_ref[0, first + k], c * step + w].astype(WIDE)
                        xs.append(x)
                        squares.append(jnp.sum(x * x, axis=0, keepdims=True))
                    energy = jnp.sum(jnp.concatenate(squares, axis=0), axis=1, keepdims=True)
                    scale = lax.rsqrt(energy / (rows * LANES) + EPSILON)
                    scale = jnp.broadcast_to(scale, (BLOCK, LANES))
                    for k, x in enumerate(xs):
                        factor = jnp.broadcast_to(scale[k : k + 1], (rows, LANES))
                        place = pl.ds(w * rows * stations + first + k, rows, stride=stations)
                        rowed[place, :] = x * factor * weight
            for piece, out in zip(PIECES, outs):
                for i, (tile, d) in enumerate(piece):
                    owner = lax.rem(here + d, hours)
                    for w in range(step):
                        start = (w * tiles + owner * mine + tile) * height
                        white = rowed[pl.ds(pl.multiple_of(start, height), height), :]
                        out[i * windows + c * step + w] = white.astype(jnp.bfloat16)

    hbm = pl.BlockSpec(memory_space=pltpu.HBM)
    inputs = (station_order, pair_blocks, band_weight, spectra)
    return pl.pallas_call(
        body,
        in_specs=[hbm] * 4,
        out_specs=[VMEM] * len(PIECES),
        out_shape=[
            jax.ShapeDtypeStruct((len(piece) * windows + 1, height, LANES), jnp.bfloat16)
            for piece in PIECES
        ],
        scratch_shapes=[
            pltpu.SMEM(station_order.shape, jnp.int32),
            pltpu.SMEM(pair_blocks.shape, jnp.int32),
            pltpu.VMEM((tiles, LANES), WIDE),
            pltpu.VMEM((rows, LANES), WIDE),
            pltpu.VMEM((step * rows * stations, LANES), WIDE),
            pltpu.VMEM(spectra.shape, jnp.bfloat16),
            pltpu.SemaphoreType.DMA((chunks,)),
            pltpu.SemaphoreType.DMA((3,)),
        ],
        compiler_params=limits(8),
        name="whiten",
    )(*[pltpu.with_memory_space_constraint(value, pltpu.HBM) for value in inputs])


def unit(first_row, own_ref, other_ref, out_ref, wide):
    stations = own_ref.shape[1] // 2
    windows = wide.shape[0]
    wide[...] = own_ref[pl.ds(first_row, windows)].astype(WIDE)
    for first in range(0, stations, BLOCK):

        def body(w, sums):
            other = other_ref[first_row + w].astype(WIDE)
            re, im = other[:stations], other[stations:]
            new = []
            for k in range(BLOCK):
                a = first + k
                a_re = jnp.broadcast_to(wide[w, a : a + 1, :], re.shape)
                a_im = jnp.broadcast_to(wide[w, stations + a : stations + a + 1, :], re.shape)
                new.append(sums[2 * k] + (a_re * re + a_im * im))
                new.append(sums[2 * k + 1] + (a_re * im - a_im * re))
            return tuple(new)

        zero = jnp.zeros((stations, LANES), WIDE)
        sums = lax.fori_loop(0, windows, body, (zero,) * (2 * BLOCK), unroll=6)
        for k in range(BLOCK):
            out_ref[first + k, :stations] = sums[2 * k].astype(out_ref.dtype)
            out_ref[first + k, stations:] = sums[2 * k + 1].astype(out_ref.dtype)


def products(pair_blocks, own, other, windows, place, dtype):
    entries, height, _ = own.shape
    stations = height // 2
    row = place * windows

    def body(pairs_ref, own_ref, other_ref, out_ref, wide, twin):
        me = lax.axis_index("sta")
        last = me == lax.axis_size("sta") - 1
        flags = other_ref[entries - 1].astype(WIDE)
        asked = jnp.logical_or(asks_itself(pairs_ref, me), jnp.max(flags) > 0.5)
        alone = jnp.logical_and(last, asked)

        @pl.when(jnp.logical_not(alone))
        def _():
            unit(row, own_ref, other_ref, out_ref, wide)

        @pl.when(alone)
        def _():
            column = lax.broadcasted_iota(jnp.int32, (stations, LANES), 0)
            for k, ref in enumerate((own_ref, other_ref)):
                unit(row, ref, ref, twin.at[k], wide)

            @pl.loop(0, stations)
            def _(a):
                one, two = twin[0, a], twin[1, a]
                re = jnp.where(column >= a, one[:stations], two[:stations])
                im = jnp.where(column >= a, one[stations:], two[stations:])
                im = jnp.where(column == a, two[:stations], im)
                out_ref[a, :stations] = re.astype(dtype)
                out_ref[a, stations:] = im.astype(dtype)

    flops = stations * stations * LANES * windows * 8
    return pl.pallas_call(
        body,
        in_specs=[SMEM, VMEM, VMEM],
        out_specs=VMEM,
        out_shape=jax.ShapeDtypeStruct((stations, height, LANES), dtype),
        scratch_shapes=[
            pltpu.VMEM((windows, height, LANES), WIDE),
            pltpu.VMEM((2, stations, height, LANES), WIDE),
        ],
        compiler_params=limits(4),
        cost_estimate=pl.CostEstimate(flops=flops, bytes_accessed=1 << 19, transcendentals=0),
        name="products",
    )(pair_blocks, own, other)


def turn(a, value, buf_ref):
    height = value.shape[0]
    stations = height // 2
    for part in range(2):
        rows = value[part * stations : (part + 1) * stations]
        buf_ref[pl.ds(part * stations + a, stations, stride=height), :] = -rows if part else rows


def add_hours(parts, owned, tiles, scale):
    stations, height, _ = parts[0].shape
    shape = (tiles, stations, height, LANES)

    def body(*refs):
        part_refs, (mine_ref, turned_ref, buf) = refs[: len(parts)], refs[len(parts) :]
        for tile in range(tiles):
            terms = [ref for ref, t in zip(part_refs, owned) if t == tile]
            for a in range(stations):
                total = terms[0][a].astype(WIDE)
                for ref in terms[1:]:
                    total = total + ref[a].astype(WIDE)
                total = total * scale
                mine_ref[tile, a] = total
                turn(a, total, buf.at[tile])
            for c in range(stations):
                rows = buf[tile, pl.ds(c * height, height), :]
                turned_ref[tile, c] = rows.astype(turned_ref.dtype)

    return pl.pallas_call(
        body,
        in_specs=[VMEM] * len(parts),
        out_specs=[VMEM] * 2,
        out_shape=[jax.ShapeDtypeStruct(shape, WIDE), jax.ShapeDtypeStruct(shape, jnp.bfloat16)],
        scratch_shapes=[pltpu.VMEM((tiles, stations * height, LANES), WIDE)],
        compiler_params=limits(4),
        name="add_hours",
    )(*parts)


def assemble(pair_blocks, mine, turned, other):
    tiles, stations, height, _ = mine.shape
    pairs = pair_blocks.shape[0]

    def body(pairs_ref, mine_ref, turned_ref, other_ref, out_ref, buf):
        me, count = lax.axis_index("sta"), lax.axis_size("sta")
        column = lax.broadcasted_iota(jnp.int32, (stations, LANES), 0)

        def put(p, a, tile, value):
            for part in range(2):
                rows = value[part * stations : (part + 1) * stations]
                out_ref[p, a, pl.ds(tile * 2 + part, stations, stride=2 * tiles), :] = rows

        def hermitian(p, a, tile, above, below, middle):
            re = jnp.where(column > a, above[:stations], below[:stations])
            im = jnp.where(column > a, above[stations:], below[stations:])
            re = jnp.where(column == a, middle, re)
            im = jnp.where(column == a, jnp.zeros_like(im), im)
            put(p, a, tile, jnp.concatenate([re, im], axis=0))

        for p in range(pairs):
            step = pairs_ref[p, 1] - me

            @pl.when(step == 1)
            def _(p=p):
                for tile in range(tiles):
                    for a in range(stations):
                        put(p, a, tile, mine_ref[tile, a])

            @pl.when(step == -1)
            def _(p=p):
                for tile in range(tiles):
                    for a in range(stations):
                        put(p, a, tile, other_ref[tile, a].astype(WIDE))

            @pl.when(jnp.logical_and(step == 0, me == count - 1))
            def _(p=p):
                for tile in range(tiles):
                    for a in range(stations):
                        own = mine_ref[tile, a]
                        back = turned_ref[tile, a].astype(WIDE)
                        hermitian(p, a, tile, own, back, own[:stations])

            @pl.when(jnp.logical_and(step == 0, me == 0))
            def _(p=p):
                for tile in range(tiles):
                    for a in range(stations):
                        turn(a, other_ref[tile, a].astype(WIDE), buf.at[tile])
                    for a in range(stations):
                        theirs = other_ref[tile, a].astype(WIDE)
                        back = buf[tile, pl.ds(a * height, height), :]
                        hermitian(p, a, tile, theirs, back, -theirs[stations:])

    rows = stations * tiles * 2
    return pl.pallas_call(
        body,
        in_specs=[SMEM, VMEM, VMEM, VMEM],
        out_specs=VMEM,
        out_shape=jax.ShapeDtypeStruct((pairs, stations, rows, LANES), WIDE),
        scratch_shapes=[pltpu.VMEM((tiles, stations * height, LANES), WIDE)],
        compiler_params=limits(4),
        name="assemble",
    )(pair_blocks, mine, turned, other)


def per_device(spectra, band_weight, station_order, pair_blocks):
    stations, _, windows, _, bins = spectra.shape
    tiles, pairs = bins // LANES, pair_blocks.shape[0]
    count, hours = lax.axis_size("sta"), lax.axis_size("hour")
    rows = spectra.reshape(stations, windows, 2, tiles, LANES)
    rows = rows.transpose(0, 1, 3, 2, 4).reshape(stations, windows, 2 * tiles, LANES)
    own = whiten(rows, band_weight.reshape(tiles, LANES), station_order, pair_blocks, hours)

    down = [((i + 1) % count, i) for i in range(count)]
    up = [(j, i) for i, j in down]
    other = [lax.ppermute(piece, "sta", down) for piece in own]
    parts, owned = [], []
    for piece, mine, theirs in zip(PIECES, own, other):
        for place, (tile, d) in enumerate(piece):
            part = products(pair_blocks, mine, theirs, windows, place, jnp.bfloat16 if d else WIDE)
            if d:
                part = lax.ppermute(part, "hour", [(h, (h + d) % hours) for h in range(hours)])
            parts.append(part)
            owned.append(tile)
    mine, turned = add_hours(parts, owned, tiles // hours, 1.0 / (hours * windows))
    theirs = lax.ppermute(turned, "sta", up)
    cross = assemble(pair_blocks, mine, turned, theirs)
    cross = cross.reshape(pairs, stations, stations, tiles // hours, 2, LANES)
    return cross.transpose(0, 1, 2, 4, 3, 5).reshape(pairs, stations, stations, 2, bins // hours)


def solution(mesh):
    return jax.shard_map(
        per_device,
        mesh=mesh,
        in_specs=(P("sta", "hour", None, None, None), P(), P("sta", None), P("sta", None)),
        out_specs=P("sta", None, None, None, "hour"),
        check_vma=False,
    )
```

```python
import jax
import jax.numpy as jnp
from jax import lax
from jax.experimental import pallas as pl
from jax.experimental.pallas import tpu as pltpu
from jax.sharding import PartitionSpec as P

LANES = 128
EPSILON = 1e-06
BLOCK = 8
ORDER = (2, 1, 3, 0)
BATCH = 2
WIDE = jnp.float32
VMEM = pl.BlockSpec(memory_space=pltpu.VMEM)


def limits(mib):
    return pltpu.CompilerParams(vmem_limit_bytes=mib << 20)


def near_tile():
    return 1 - lax.rem(lax.axis_index("sta"), 2)


def whiten(spectra, band_weight, station_order, pair_blocks, hours):
    stations, windows, rows, _ = spectra.shape
    tiles = rows // 2
    mine = tiles // hours
    chunks = 5
    step = windows // chunks
    batches = hours // BATCH
    height = 2 * stations

    def body(order_hbm, pairs_hbm, band_hbm, x_hbm, *refs):
        near_refs, (far_ref, steps_ref) = refs[:batches], refs[batches : batches + 2]
        order_ref, pairs_ref, band_ref, band, rowed, x_ref, sems, small = refs[batches + 2 :]

        def fetch(c):
            part = pl.ds(c * step, step)
            return pltpu.make_async_copy(x_hbm.at[:, part], x_ref.at[:, part], sems.at[c])

        fetch(0).start()
        copies = [
            pltpu.make_async_copy(order_hbm, order_ref, small.at[0]),
            pltpu.make_async_copy(pairs_hbm, pairs_ref, small.at[1]),
            pltpu.make_async_copy(band_hbm, band_ref, small.at[2]),
        ]
        for copy in copies:
            copy.start()
        for c in range(1, chunks):
            fetch(c).start()
        for copy in copies:
            copy.wait()
        for part in range(2):
            band[pl.ds(part, tiles, stride=2), :] = band_ref[...]
        weight = band[...]
        here, me, near = lax.axis_index("hour"), lax.axis_index("sta"), near_tile()
        asked = pairs_ref[0, 1] == me
        for p in range(pair_blocks.shape[0]):
            asked = jnp.logical_or(asked, pairs_ref[p, 1] == me)
            away = (pairs_ref[p, 1] - me).astype(WIDE)
            steps_ref[p] = jnp.full((8, LANES), away, WIDE)
        flag = jnp.where(asked, 1.0, 0.0)
        far_ref[hours * windows] = jnp.full((height, LANES), flag, WIDE).astype(jnp.bfloat16)

        @pl.loop(0, chunks)
        def _(c):
            fetch(c).wait()
            for w in range(step):
                for first in range(0, stations, BLOCK):
                    xs, squares = [], []
                    for k in range(BLOCK):
                        x = x_ref[order_ref[0, first + k], c * step + w].astype(WIDE)
                        xs.append(x)
                        squares.append(jnp.sum(x * x, axis=0, keepdims=True))
                    energy = jnp.sum(jnp.concatenate(squares, axis=0), axis=1, keepdims=True)
                    scale = lax.rsqrt(energy / (rows * LANES) + EPSILON)
                    scale = jnp.broadcast_to(scale, (BLOCK, LANES))
                    for k, x in enumerate(xs):
                        factor = jnp.broadcast_to(scale[k : k + 1], (rows, LANES))
                        place = pl.ds(w * rows * stations + first + k, rows, stride=stations)
                        rowed[place, :] = x * factor * weight
            for k, d in enumerate(ORDER):
                owner = lax.rem(here + d, hours)
                for w in range(step):
                    for tile, out, row in ((near, near_refs[k // BATCH], k % BATCH), (1 - near, far_ref, k)):
                        start = (w * tiles + owner * mine + tile) * height
                        white = rowed[pl.ds(pl.multiple_of(start, height), height), :]
                        out[row * windows + c * step + w] = white.astype(jnp.bfloat16)

    hbm = pl.BlockSpec(memory_space=pltpu.HBM)
    inputs = (station_order, pair_blocks, band_weight, spectra)
    outs = pl.pallas_call(
        body,
        in_specs=[hbm] * 4,
        out_specs=[VMEM] * (batches + 2),
        out_shape=[jax.ShapeDtypeStruct((BATCH * windows, height, LANES), jnp.bfloat16)] * batches
        + [
            jax.ShapeDtypeStruct((hours * windows + 1, height, LANES), jnp.bfloat16),
            jax.ShapeDtypeStruct((pair_blocks.shape[0], 8, LANES), WIDE),
        ],
        scratch_shapes=[
            pltpu.SMEM(station_order.shape, jnp.int32),
            pltpu.SMEM(pair_blocks.shape, jnp.int32),
            pltpu.VMEM((tiles, LANES), WIDE),
            pltpu.VMEM((rows, LANES), WIDE),
            pltpu.VMEM((step * rows * stations, LANES), WIDE),
            pltpu.VMEM(spectra.shape, jnp.bfloat16),
            pltpu.SemaphoreType.DMA((chunks,)),
            pltpu.SemaphoreType.DMA((3,)),
        ],
        compiler_params=limits(8),
        name="whiten",
    )(*[pltpu.with_memory_space_constraint(value, pltpu.HBM) for value in inputs])
    return outs[:batches], outs[batches], outs[batches + 1]


def unit(own_ref, own_row, other_ref, other_row, out_ref, wide):
    stations = own_ref.shape[1] // 2
    windows = wide.shape[0]
    wide[...] = own_ref[pl.ds(own_row, windows)].astype(WIDE)
    for first in range(0, stations, BLOCK):

        def body(w, sums):
            other = other_ref[other_row + w].astype(WIDE)
            re, im = other[:stations], other[stations:]
            new = []
            for k in range(BLOCK):
                a = first + k
                a_re = jnp.broadcast_to(wide[w, a : a + 1, :], re.shape)
                a_im = jnp.broadcast_to(wide[w, stations + a : stations + a + 1, :], re.shape)
                new.append(sums[2 * k] + (a_re * re + a_im * im))
                new.append(sums[2 * k + 1] + (a_re * im - a_im * re))
            return tuple(new)

        zero = jnp.zeros((stations, LANES), WIDE)
        sums = lax.fori_loop(0, windows, body, (zero,) * (2 * BLOCK), unroll=6)
        for k in range(BLOCK):
            out_ref[first + k, :stations] = sums[2 * k].astype(out_ref.dtype)
            out_ref[first + k, stations:] = sums[2 * k + 1].astype(out_ref.dtype)


def product_call(body, operands, windows, dtype, scratch_shapes):
    height = operands[0].shape[1]
    stations = height // 2
    return pl.pallas_call(
        body,
        in_specs=[VMEM] * len(operands),
        out_specs=VMEM,
        out_shape=jax.ShapeDtypeStruct((stations, height, LANES), dtype),
        scratch_shapes=[pltpu.VMEM((windows, height, LANES), WIDE)] + scratch_shapes,
        compiler_params=limits(4),
        cost_estimate=pl.CostEstimate(
            flops=stations * stations * LANES * windows * 8, bytes_accessed=1 << 19, transcendentals=0
        ),
        name="products",
    )(*operands)


def near_product(own, own_place, others, place, windows, dtype):
    def body(own_ref, other_ref, out_ref, wide):
        unit(own_ref, own_place * windows, other_ref, place * windows, out_ref, wide)

    return product_call(body, (own, others), windows, dtype, [])


def far_product(owns, place, other, near, near_place, windows, dtype):
    _, height, _ = other.shape
    stations = height // 2
    row, near_row = place * windows, near_place * windows

    def body(own_ref, other_ref, near_ref, out_ref, wide, twin):
        me = lax.axis_index("sta")
        end = jnp.logical_or(me == 0, me == lax.axis_size("sta") - 1)
        flags = own_ref[owns.shape[0] - 1, :8].astype(WIDE)
        alone = jnp.logical_and(end, jnp.max(flags) > 0.5)

        @pl.when(jnp.logical_not(alone))
        def _():
            unit(own_ref, row, other_ref, near_row, out_ref, wide)

        @pl.when(alone)
        def _():
            unit(own_ref, row, own_ref, row, twin.at[0], wide)
            unit(near_ref, near_row, near_ref, near_row, twin.at[1], wide)
            column = lax.broadcasted_iota(jnp.int32, (stations, LANES), 0)

            @pl.loop(0, stations)
            def _(a):
                one, two = twin[0, a], twin[1, a]
                re = jnp.where(column >= a, one[:stations], two[:stations])
                im = jnp.where(column >= a, one[stations:], two[stations:])
                im = jnp.where(column == a, two[:stations], im)
                out_ref[a, :stations] = re.astype(dtype)
                out_ref[a, stations:] = im.astype(dtype)

    twin = pltpu.VMEM((2, stations, height, LANES), WIDE)
    return product_call(body, (owns, other, near), windows, dtype, [twin])


def turn(a, value, buf_ref):
    height = value.shape[0]
    stations = height // 2
    for part in range(2):
        rows = value[part * stations : (part + 1) * stations]
        buf_ref[pl.ds(part * stations + a, stations, stride=height), :] = -rows if part else rows


def add_hours(parts, scale):
    shape = parts[0].shape
    stations, height, _ = shape

    def body(*refs):
        part_refs, (mine_ref, turned_ref, buf) = refs[: len(parts)], refs[len(parts) :]
        for a in range(stations):
            total = part_refs[0][a].astype(WIDE)
            for ref in part_refs[1:]:
                total = total + ref[a].astype(WIDE)
            total = total * scale
            mine_ref[a] = total
            turn(a, total, buf)
        for c in range(stations):
            turned_ref[c] = buf[pl.ds(c * height, height), :].astype(turned_ref.dtype)

    return pl.pallas_call(
        body,
        in_specs=[VMEM] * len(parts),
        out_specs=[VMEM] * 2,
        out_shape=[jax.ShapeDtypeStruct(shape, WIDE), jax.ShapeDtypeStruct(shape, jnp.bfloat16)],
        scratch_shapes=[pltpu.VMEM((stations * height, LANES), WIDE)],
        compiler_params=limits(4),
        name="add_hours",
    )(*parts)


def assemble(steps, near, far, turned):
    stations, height, _ = turned.shape
    pairs, tiles = steps.shape[0], 2

    def body(steps_ref, near_mine, near_theirs, far_mine, far_theirs, turned_ref, out_ref):
        first = near_tile()
        column = lax.broadcasted_iota(jnp.int32, (stations, LANES), 0)

        def put(p, a, tile, value):
            for part in range(2):
                rows = value[part * stations : (part + 1) * stations]
                out_ref[p, a, pl.ds(tile * 2 + part, stations, stride=2 * tiles), :] = rows

        def hermitian(p, a, tile, above, below, middle):
            re = jnp.where(column > a, above[:stations], below[:stations])
            im = jnp.where(column > a, above[stations:], below[stations:])
            re = jnp.where(column == a, middle, re)
            im = jnp.where(column == a, jnp.zeros_like(im), im)
            put(p, a, tile, jnp.concatenate([re, im], axis=0))

        for p in range(pairs):
            away = jnp.max(steps_ref[p])
            alone = jnp.abs(away) < 0.5
            inside = jnp.logical_and((away > 0.5) == (first == 1), jnp.logical_not(alone))
            outside = jnp.logical_not(jnp.logical_or(alone, inside))

            @pl.when(inside)
            def _(p=p):
                for a in range(stations):
                    put(p, a, first, near_mine[a])
                    put(p, a, 1 - first, near_theirs[a].astype(WIDE))

            @pl.when(outside)
            def _(p=p):
                for a in range(stations):
                    put(p, a, 1 - first, far_mine[a])
                    put(p, a, first, far_theirs[a].astype(WIDE))

            @pl.when(alone)
            def _(p=p):
                for a in range(stations):
                    own, back = far_mine[a], turned_ref[a].astype(WIDE)
                    hermitian(p, a, 1 - first, own, back, own[:stations])
                    hermitian(p, a, first, back, own, own[stations:])

    return pl.pallas_call(
        body,
        in_specs=[VMEM] * 6,
        out_specs=VMEM,
        out_shape=jax.ShapeDtypeStruct((pairs, stations, stations * tiles * 2, LANES), WIDE),
        compiler_params=limits(4),
        name="assemble",
    )(steps, *near, *far, turned)


def per_device(spectra, band_weight, station_order, pair_blocks):
    stations, _, windows, _, bins = spectra.shape
    tiles, pairs = bins // LANES, pair_blocks.shape[0]
    count, hours = lax.axis_size("sta"), lax.axis_size("hour")
    rows = spectra.reshape(stations, windows, 2, tiles, LANES)
    rows = rows.transpose(0, 1, 3, 2, 4).reshape(stations, windows, 2 * tiles, LANES)
    near, far, steps = whiten(rows, band_weight.reshape(tiles, LANES), station_order, pair_blocks, hours)

    on_chip = [(g, g ^ 1) for g in range(count)]
    across = [(g, h) for i in range(1, count - 1, 2) for g, h in ((i, i + 1), (i + 1, i))]

    def to_owner(part, d):
        return lax.ppermute(part, "hour", [(h, (h + d) % hours) for h in range(hours)]) if d else part

    def after(value, *earlier):
        return lax.optimization_barrier((value, earlier))[0]

    near_others = lax.ppermute(far, "sta", on_chip)
    far_others = [lax.ppermute(one, "sta", across) for one in near]
    dtypes = [jnp.bfloat16 if d else WIDE for d in ORDER]
    scale = 1.0 / (hours * windows)

    near_made = [
        near_product(near[k // BATCH], k % BATCH, near_others, k, windows, dtypes[k])
        for k in range(hours)
    ]
    near_parts = [to_owner(part, d) for part, d in zip(near_made, ORDER)]
    far_others[0] = after(far_others[0], *near_made)
    far_made = []
    for k in range(hours):
        batch, place = divmod(k, BATCH)
        if k == (hours // BATCH - 1) * BATCH:
            near_mine, turned = add_hours(after(near_parts, *far_made), scale)
            near_theirs = lax.ppermute(turned, "sta", on_chip)
            far_others[batch] = after(far_others[batch], near_mine)
        far_made.append(far_product(far, k, far_others[batch], near[batch], place, windows, dtypes[k]))
    far_parts = [to_owner(part, d) for part, d in zip(far_made, ORDER)]
    far_mine, turned = add_hours(far_parts, scale)
    far_theirs = lax.ppermute(turned, "sta", across)
    cross = assemble(steps, (near_mine, near_theirs), (far_mine, far_theirs), turned)
    cross = cross.reshape(pairs, stations, stations, tiles // hours, 2, LANES)
    return cross.transpose(0, 1, 2, 4, 3, 5).reshape(pairs, stations, stations, 2, bins // hours)


def solution(mesh):
    return jax.shard_map(
        per_device,
        mesh=mesh,
        in_specs=(P("sta", "hour", None, None, None), P(), P("sta", None), P("sta", None)),
        out_specs=P("sta", None, None, None, "hour"),
        check_vma=False,
    )
```

```python
import jax
import jax.numpy as jnp
from jax import lax
from jax.experimental import pallas as pl
from jax.experimental.pallas import tpu as pltpu
from jax.sharding import PartitionSpec as P

LANES = 128
EPSILON = 1e-06
BLOCK = 8
ORDER = (2, 1, 3, 0)
BATCH = 2
WIDE = jnp.float32
VMEM = pl.BlockSpec(memory_space=pltpu.VMEM)


def limits(mib):
    return pltpu.CompilerParams(vmem_limit_bytes=mib << 20)


def whiten(spectra, band_weight, station_order, pair_blocks, hours):
    stations, windows, rows, _ = spectra.shape
    tiles = rows // 2
    mine = tiles // hours
    chunks = 5
    step = windows // chunks
    batches = hours // BATCH
    height = 2 * stations

    def body(order_hbm, pairs_hbm, band_hbm, x_hbm, *refs):
        piece_refs, (whole_ref, steps_ref) = refs[:batches], refs[batches : batches + 2]
        order_ref, pairs_ref, band_ref, band, rowed, x_ref, sems, small = refs[batches + 2 :]

        def fetch(c):
            part = pl.ds(c * step, step)
            return pltpu.make_async_copy(x_hbm.at[:, part], x_ref.at[:, part], sems.at[c])

        fetch(0).start()
        copies = [
            pltpu.make_async_copy(order_hbm, order_ref, small.at[0]),
            pltpu.make_async_copy(pairs_hbm, pairs_ref, small.at[1]),
            pltpu.make_async_copy(band_hbm, band_ref, small.at[2]),
        ]
        for copy in copies:
            copy.start()
        for c in range(1, chunks):
            fetch(c).start()
        for copy in copies:
            copy.wait()
        for part in range(2):
            band[pl.ds(part, tiles, stride=2), :] = band_ref[...]
        weight = band[...]
        here, me = lax.axis_index("hour"), lax.axis_index("sta")
        even = lax.rem(me, 2) == 0
        asked = pairs_ref[0, 1] == me
        for p in range(pair_blocks.shape[0]):
            asked = jnp.logical_or(asked, pairs_ref[p, 1] == me)
            away = (pairs_ref[p, 1] - me).astype(WIDE)
            steps_ref[p] = jnp.full((8, LANES), away, WIDE)
        flag = jnp.where(asked, 1.0, 0.0)
        for out in (*piece_refs, whole_ref):
            out[out.shape[0] - 1] = jnp.full((height, LANES), flag, WIDE).astype(jnp.bfloat16)

        @pl.loop(0, chunks)
        def _(c):
            fetch(c).wait()
            for w in range(step):
                for first in range(0, stations, BLOCK):
                    xs, squares = [], []
                    for k in range(BLOCK):
                        x = x_ref[order_ref[0, first + k], c * step + w].astype(WIDE)
                        xs.append(x)
                        squares.append(jnp.sum(x * x, axis=0, keepdims=True))
                    energy = jnp.sum(jnp.concatenate(squares, axis=0), axis=1, keepdims=True)
                    scale = lax.rsqrt(energy / (rows * LANES) + EPSILON)
                    scale = jnp.broadcast_to(scale, (BLOCK, LANES))
                    for k, x in enumerate(xs):
                        factor = jnp.broadcast_to(scale[k : k + 1], (rows, LANES))
                        place = pl.ds(w * rows * stations + first + k, rows, stride=stations)
                        rowed[place, :] = x * factor * weight

            def write(k, out, row):
                owner = lax.rem(here + ORDER[k], hours)
                for tile in range(mine):
                    for w in range(step):
                        start = (w * tiles + owner * mine + tile) * height
                        white = rowed[pl.ds(pl.multiple_of(start, height), height), :]
                        out[row + tile * windows + c * step + w] = white.astype(jnp.bfloat16)

            @pl.when(even)
            def _():
                for k in range(hours):
                    write(k, piece_refs[k // BATCH], k % BATCH * mine * windows)

            @pl.when(jnp.logical_not(even))
            def _():
                for k in range(hours):
                    write(k, whole_ref, k * mine * windows)

    hbm = pl.BlockSpec(memory_space=pltpu.HBM)
    inputs = (station_order, pair_blocks, band_weight, spectra)
    outs = pl.pallas_call(
        body,
        in_specs=[hbm] * 4,
        out_specs=[VMEM] * (batches + 2),
        out_shape=[jax.ShapeDtypeStruct((BATCH * mine * windows + 1, height, LANES), jnp.bfloat16)] * batches
        + [
            jax.ShapeDtypeStruct((tiles * windows + 1, height, LANES), jnp.bfloat16),
            jax.ShapeDtypeStruct((pair_blocks.shape[0], 8, LANES), WIDE),
        ],
        scratch_shapes=[
            pltpu.SMEM(station_order.shape, jnp.int32),
            pltpu.SMEM(pair_blocks.shape, jnp.int32),
            pltpu.VMEM((tiles, LANES), WIDE),
            pltpu.VMEM((rows, LANES), WIDE),
            pltpu.VMEM((step * rows * stations, LANES), WIDE),
            pltpu.VMEM(spectra.shape, jnp.bfloat16),
            pltpu.SemaphoreType.DMA((chunks,)),
            pltpu.SemaphoreType.DMA((3,)),
        ],
        compiler_params=limits(8),
        name="whiten",
    )(*[pltpu.with_memory_space_constraint(value, pltpu.HBM) for value in inputs])
    return outs[:batches], outs[batches], outs[batches + 1]


def unit(own_ref, own_row, other_ref, other_row, out_ref, wide):
    stations = own_ref.shape[1] // 2
    windows = wide.shape[0]
    wide[...] = own_ref[pl.ds(own_row, windows)].astype(WIDE)
    for first in range(0, stations, BLOCK):

        def body(w, sums):
            other = other_ref[other_row + w].astype(WIDE)
            re, im = other[:stations], other[stations:]
            new = []
            for k in range(BLOCK):
                a = first + k
                a_re = jnp.broadcast_to(wide[w, a : a + 1, :], re.shape)
                a_im = jnp.broadcast_to(wide[w, stations + a : stations + a + 1, :], re.shape)
                new.append(sums[2 * k] + (a_re * re + a_im * im))
                new.append(sums[2 * k + 1] + (a_re * im - a_im * re))
            return tuple(new)

        zero = jnp.zeros((stations, LANES), WIDE)
        sums = lax.fori_loop(0, windows, body, (zero,) * (2 * BLOCK), unroll=6)
        for k in range(BLOCK):
            out_ref[first + k, :stations] = sums[2 * k].astype(out_ref.dtype)
            out_ref[first + k, stations:] = sums[2 * k + 1].astype(out_ref.dtype)


def product_call(body, operands, tiles, windows, dtype, scratch_shapes):
    height = operands[0].shape[1]
    stations = height // 2
    flops = tiles * stations * stations * LANES * windows * 8
    return pl.pallas_call(
        body,
        in_specs=[VMEM] * len(operands),
        out_specs=VMEM,
        out_shape=jax.ShapeDtypeStruct((tiles, stations, height, LANES), dtype),
        scratch_shapes=[pltpu.VMEM((windows, height, LANES), WIDE)] + scratch_shapes,
        compiler_params=limits(4),
        cost_estimate=pl.CostEstimate(flops=flops, bytes_accessed=1 << 20, transcendentals=0),
        name="products",
    )(*operands)


def near_product(piece, piece_place, others, place, tiles, windows, dtype):
    def body(own_ref, other_ref, out_ref, wide):
        @pl.when(lax.rem(lax.axis_index("sta"), 2) == 0)
        def _():
            for tile in range(tiles):
                row = (place * tiles + tile) * windows
                own_row = (piece_place * tiles + tile) * windows
                unit(own_ref, own_row, other_ref, row, out_ref.at[tile], wide)

    return product_call(body, (piece, others), tiles, windows, dtype, [])


def far_product(whole, place, piece, piece_place, tiles, windows, dtype):
    entries, height, _ = piece.shape
    stations = height // 2

    def body(own_ref, other_ref, out_ref, wide, twin):
        me = lax.axis_index("sta")
        flags = own_ref[whole.shape[0] - 1, :8].astype(WIDE) + other_ref[entries - 1, :8].astype(WIDE)
        last = me == lax.axis_size("sta") - 1
        alone = jnp.logical_and(last, jnp.max(flags) > 0.5)

        @pl.when(jnp.logical_and(lax.rem(me, 2) == 1, jnp.logical_not(alone)))
        def _():
            for tile in range(tiles):
                row = (place * tiles + tile) * windows
                other_row = (piece_place * tiles + tile) * windows
                unit(own_ref, row, other_ref, other_row, out_ref.at[tile], wide)

        @pl.when(alone)
        def _():
            column = lax.broadcasted_iota(jnp.int32, (stations, LANES), 0)
            for tile in range(tiles):
                row = (place * tiles + tile) * windows
                unit(own_ref, row, own_ref, row, twin.at[0], wide)
                other_row = (piece_place * tiles + tile) * windows
                unit(other_ref, other_row, other_ref, other_row, twin.at[1], wide)

                @pl.loop(0, stations)
                def _(a, tile=tile):
                    one, two = twin[0, a], twin[1, a]
                    re = jnp.where(column >= a, one[:stations], two[:stations])
                    im = jnp.where(column >= a, one[stations:], two[stations:])
                    im = jnp.where(column == a, two[:stations], im)
                    out_ref[tile, a, :stations] = re.astype(dtype)
                    out_ref[tile, a, stations:] = im.astype(dtype)

    twin = pltpu.VMEM((2, stations, height, LANES), WIDE)
    return product_call(body, (whole, piece), tiles, windows, dtype, [twin])


def turn(a, value, buf_ref):
    height = value.shape[0]
    stations = height // 2
    for part in range(2):
        rows = value[part * stations : (part + 1) * stations]
        buf_ref[pl.ds(part * stations + a, stations, stride=height), :] = -rows if part else rows


def add_hours(parts, parity, scale):
    shape = parts[0].shape
    tiles, stations, height, _ = shape

    def body(*refs):
        part_refs, (mine_ref, turned_ref, buf) = refs[: len(parts)], refs[len(parts) :]

        @pl.when(lax.rem(lax.axis_index("sta"), 2) == parity)
        def _():
            for tile in range(tiles):
                for a in range(stations):
                    total = part_refs[0][tile, a].astype(WIDE)
                    for ref in part_refs[1:]:
                        total = total + ref[tile, a].astype(WIDE)
                    total = total * scale
                    mine_ref[tile, a] = total
                    turn(a, total, buf.at[tile])
                for c in range(stations):
                    rows = buf[tile, pl.ds(c * height, height), :]
                    turned_ref[tile, c] = rows.astype(turned_ref.dtype)

    return pl.pallas_call(
        body,
        in_specs=[VMEM] * len(parts),
        out_specs=[VMEM] * 2,
        out_shape=[jax.ShapeDtypeStruct(shape, WIDE), jax.ShapeDtypeStruct(shape, jnp.bfloat16)],
        scratch_shapes=[pltpu.VMEM((tiles, stations * height, LANES), WIDE)],
        compiler_params=limits(4),
        name="add_hours",
    )(*parts)


def assemble(steps, near, far, turned):
    tiles, stations, height, _ = turned.shape
    pairs = steps.shape[0]

    def body(steps_ref, near_mine, near_theirs, far_mine, far_theirs, turned_ref, out_ref, buf):
        me = lax.axis_index("sta")
        even = lax.rem(me, 2) == 0
        odd = jnp.logical_not(even)
        column = lax.broadcasted_iota(jnp.int32, (stations, LANES), 0)

        def put(p, a, tile, value):
            for part in range(2):
                rows = value[part * stations : (part + 1) * stations]
                out_ref[p, a, pl.ds(tile * 2 + part, stations, stride=2 * tiles), :] = rows

        def hermitian(p, a, tile, above, below, middle):
            re = jnp.where(column > a, above[:stations], below[:stations])
            im = jnp.where(column > a, above[stations:], below[stations:])
            re = jnp.where(column == a, middle, re)
            im = jnp.where(column == a, jnp.zeros_like(im), im)
            put(p, a, tile, jnp.concatenate([re, im], axis=0))

        for p in range(pairs):
            away = jnp.max(steps_ref[p])
            before, after, alone = away < -0.5, away > 0.5, jnp.abs(away) < 0.5
            cases = (
                (jnp.logical_and(even, after), near_mine),
                (jnp.logical_and(odd, before), near_theirs),
                (jnp.logical_and(odd, after), far_mine),
                (jnp.logical_and(even, before), far_theirs),
            )
            for case, ref in cases:

                @pl.when(case)
                def _(p=p, ref=ref):
                    for tile in range(tiles):
                        for a in range(stations):
                            put(p, a, tile, ref[tile, a].astype(WIDE))

            @pl.when(jnp.logical_and(odd, alone))
            def _(p=p):
                for tile in range(tiles):
                    for a in range(stations):
                        own = far_mine[tile, a]
                        back = turned_ref[tile, a].astype(WIDE)
                        hermitian(p, a, tile, own, back, own[:stations])

            @pl.when(jnp.logical_and(even, alone))
            def _(p=p):
                for tile in range(tiles):
                    for a in range(stations):
                        turn(a, far_theirs[tile, a].astype(WIDE), buf)
                    for a in range(stations):
                        theirs = far_theirs[tile, a].astype(WIDE)
                        back = buf[pl.ds(a * height, height), :]
                        hermitian(p, a, tile, theirs, back, -theirs[stations:])

    return pl.pallas_call(
        body,
        in_specs=[VMEM] * 6,
        out_specs=VMEM,
        out_shape=jax.ShapeDtypeStruct((pairs, stations, stations * tiles * 2, LANES), WIDE),
        scratch_shapes=[pltpu.VMEM((stations * height, LANES), WIDE)],
        compiler_params=limits(4),
        name="assemble",
    )(steps, *near, *far, turned)


def per_device(spectra, band_weight, station_order, pair_blocks):
    stations, _, windows, _, bins = spectra.shape
    tiles, pairs = bins // LANES, pair_blocks.shape[0]
    count, hours = lax.axis_size("sta"), lax.axis_size("hour")
    rows = spectra.reshape(stations, windows, 2, tiles, LANES)
    rows = rows.transpose(0, 1, 3, 2, 4).reshape(stations, windows, 2 * tiles, LANES)
    pieces, whole, steps = whiten(rows, band_weight.reshape(tiles, LANES), station_order, pair_blocks, hours)

    near_pairs = [(g + 1, g) for g in range(0, count, 2)]
    far_pairs = [((g + 1) % count, g) for g in range(1, count, 2)]

    def back(pairs):
        return [(j, i) for i, j in pairs]

    def to_owner(part, d, parity):
        if d == 0:
            return part
        moves = [
            (g * hours + h, g * hours + (h + d) % hours)
            for g in range(parity, count, 2)
            for h in range(hours)
        ]
        return lax.ppermute(part, ("sta", "hour"), moves)

    def after(value, *earlier):
        return lax.optimization_barrier((value, earlier))[0]

    dtypes = [jnp.bfloat16 if d else WIDE for d in ORDER]
    scale = 1.0 / (hours * windows)
    near_others = lax.ppermute(whole, "sta", near_pairs)
    far_others = [lax.ppermute(piece, "sta", far_pairs) for piece in pieces]
    mine = tiles // hours
    near_made, far_made = [], []
    for k in range(hours):
        batch, place = divmod(k, BATCH)
        near_made.append(near_product(pieces[batch], place, near_others, k, mine, windows, dtypes[k]))
    near_parts = [to_owner(part, d, 0) for part, d in zip(near_made, ORDER)]
    far_others[0] = after(far_others[0], *near_made)
    for k in range(hours):
        batch, place = divmod(k, BATCH)
        if k == hours - BATCH:
            near_mine, turned = add_hours(after(near_parts, *far_made), 0, scale)
            near_theirs = lax.ppermute(turned, "sta", back(near_pairs))
            far_others[batch] = after(far_others[batch], near_mine)
        far_made.append(far_product(whole, k, far_others[batch], place, mine, windows, dtypes[k]))
    far_parts = [to_owner(part, d, 1) for part, d in zip(far_made, ORDER)]
    far_mine, turned = add_hours(far_parts, 1, scale)
    far_theirs = lax.ppermute(turned, "sta", back(far_pairs))
    cross = assemble(steps, (near_mine, near_theirs), (far_mine, far_theirs), turned)
    cross = cross.reshape(pairs, stations, stations, tiles // hours, 2, LANES)
    return cross.transpose(0, 1, 2, 4, 3, 5).reshape(pairs, stations, stations, 2, bins // hours)


def solution(mesh):
    return jax.shard_map(
        per_device,
        mesh=mesh,
        in_specs=(P("sta", "hour", None, None, None), P(), P("sta", None), P("sta", None)),
        out_specs=P("sta", None, None, None, "hour"),
        check_vma=False,
    )
```

```python
import jax
import jax.numpy as jnp
from jax import lax
from jax.experimental import pallas as pl
from jax.experimental.pallas import tpu as pltpu
from jax.sharding import PartitionSpec as P

LANES = 128
EPSILON = 1e-06
BLOCK = 8
ORDER = (2, 1, 3, 0)
BATCH = 2
WIDE = jnp.float32
VMEM = pl.BlockSpec(memory_space=pltpu.VMEM)


def limits(mib):
    return pltpu.CompilerParams(vmem_limit_bytes=mib << 20)


def near_tile():
    return 1 - lax.rem(lax.axis_index("sta"), 2)


def whiten(spectra, band_weight, station_order, pair_blocks, hours):
    stations, windows, rows, _ = spectra.shape
    tiles = rows // 2
    mine = tiles // hours
    chunks = 5
    step = windows // chunks
    batches = hours // BATCH
    height = 2 * stations

    def body(order_hbm, pairs_hbm, band_hbm, x_hbm, *refs):
        near_refs, (far_ref, steps_ref) = refs[:batches], refs[batches : batches + 2]
        order_ref, pairs_ref, band_ref, band, rowed, x_ref, sems, small = refs[batches + 2 :]

        def fetch(c):
            part = pl.ds(c * step, step)
            return pltpu.make_async_copy(x_hbm.at[:, part], x_ref.at[:, part], sems.at[c])

        fetch(0).start()
        copies = [
            pltpu.make_async_copy(order_hbm, order_ref, small.at[0]),
            pltpu.make_async_copy(pairs_hbm, pairs_ref, small.at[1]),
            pltpu.make_async_copy(band_hbm, band_ref, small.at[2]),
        ]
        for copy in copies:
            copy.start()
        for c in range(1, chunks):
            fetch(c).start()
        for copy in copies:
            copy.wait()
        for part in range(2):
            band[pl.ds(part, tiles, stride=2), :] = band_ref[...]
        weight = band[...]
        here, me, near = lax.axis_index("hour"), lax.axis_index("sta"), near_tile()
        asked = pairs_ref[0, 1] == me
        for p in range(pair_blocks.shape[0]):
            asked = jnp.logical_or(asked, pairs_ref[p, 1] == me)
            away = (pairs_ref[p, 1] - me).astype(WIDE)
            steps_ref[p] = jnp.full((8, LANES), away, WIDE)
        flag = jnp.where(asked, 1.0, 0.0)
        far_ref[hours * windows] = jnp.full((height, LANES), flag, WIDE).astype(jnp.bfloat16)

        @pl.loop(0, chunks)
        def _(c):
            fetch(c).wait()
            for w in range(step):
                for first in range(0, stations, BLOCK):
                    xs, squares = [], []
                    for k in range(BLOCK):
                        x = x_ref[order_ref[0, first + k], c * step + w].astype(WIDE)
                        xs.append(x)
                        squares.append(jnp.sum(x * x, axis=0, keepdims=True))
                    energy = jnp.sum(jnp.concatenate(squares, axis=0), axis=1, keepdims=True)
                    scale = lax.rsqrt(energy / (rows * LANES) + EPSILON)
                    scale = jnp.broadcast_to(scale, (BLOCK, LANES))
                    for k, x in enumerate(xs):
                        factor = jnp.broadcast_to(scale[k : k + 1], (rows, LANES))
                        place = pl.ds(w * rows * stations + first + k, rows, stride=stations)
                        rowed[place, :] = x * factor * weight
            for k, d in enumerate(ORDER):
                owner = lax.rem(here + d, hours)
                for w in range(step):
                    for tile, out, row in ((near, near_refs[k // BATCH], k % BATCH), (1 - near, far_ref, k)):
                        start = (w * tiles + owner * mine + tile) * height
                        white = rowed[pl.ds(pl.multiple_of(start, height), height), :]
                        out[row * windows + c * step + w] = white.astype(jnp.bfloat16)

    hbm = pl.BlockSpec(memory_space=pltpu.HBM)
    inputs = (station_order, pair_blocks, band_weight, spectra)
    outs = pl.pallas_call(
        body,
        in_specs=[hbm] * 4,
        out_specs=[VMEM] * (batches + 2),
        out_shape=[jax.ShapeDtypeStruct((BATCH * windows, height, LANES), jnp.bfloat16)] * batches
        + [
            jax.ShapeDtypeStruct((hours * windows + 1, height, LANES), jnp.bfloat16),
            jax.ShapeDtypeStruct((pair_blocks.shape[0], 8, LANES), WIDE),
        ],
        scratch_shapes=[
            pltpu.SMEM(station_order.shape, jnp.int32),
            pltpu.SMEM(pair_blocks.shape, jnp.int32),
            pltpu.VMEM((tiles, LANES), WIDE),
            pltpu.VMEM((rows, LANES), WIDE),
            pltpu.VMEM((step * rows * stations, LANES), WIDE),
            pltpu.VMEM(spectra.shape, jnp.bfloat16),
            pltpu.SemaphoreType.DMA((chunks,)),
            pltpu.SemaphoreType.DMA((3,)),
        ],
        compiler_params=limits(8),
        name="whiten",
    )(*[pltpu.with_memory_space_constraint(value, pltpu.HBM) for value in inputs])
    return outs[:batches], outs[batches], outs[batches + 1]


def unit(own_ref, own_row, other_ref, other_row, out_ref, wide):
    stations = own_ref.shape[1] // 2
    windows = wide.shape[0]
    wide[...] = own_ref[pl.ds(own_row, windows)].astype(WIDE)
    for first in range(0, stations, BLOCK):

        def body(w, sums):
            other = other_ref[other_row + w].astype(WIDE)
            re, im = other[:stations], other[stations:]
            new = []
            for k in range(BLOCK):
                a = first + k
                a_re = jnp.broadcast_to(wide[w, a : a + 1, :], re.shape)
                a_im = jnp.broadcast_to(wide[w, stations + a : stations + a + 1, :], re.shape)
                new.append(sums[2 * k] + (a_re * re + a_im * im))
                new.append(sums[2 * k + 1] + (a_re * im - a_im * re))
            return tuple(new)

        zero = jnp.zeros((stations, LANES), WIDE)
        sums = lax.fori_loop(0, windows, body, (zero,) * (2 * BLOCK), unroll=6)
        for k in range(BLOCK):
            out_ref[first + k, :stations] = sums[2 * k].astype(out_ref.dtype)
            out_ref[first + k, stations:] = sums[2 * k + 1].astype(out_ref.dtype)


def product_call(body, operands, windows, dtype, scratch_shapes):
    height = operands[0].shape[1]
    stations = height // 2
    return pl.pallas_call(
        body,
        in_specs=[VMEM] * len(operands),
        out_specs=VMEM,
        out_shape=jax.ShapeDtypeStruct((stations, height, LANES), dtype),
        scratch_shapes=[pltpu.VMEM((windows, height, LANES), WIDE)] + scratch_shapes,
        compiler_params=limits(4),
        cost_estimate=pl.CostEstimate(
            flops=stations * stations * LANES * windows * 8, bytes_accessed=1 << 19, transcendentals=0
        ),
        name="products",
    )(*operands)


def near_product(own, own_place, others, place, windows, dtype):
    def body(own_ref, other_ref, out_ref, wide):
        unit(own_ref, own_place * windows, other_ref, place * windows, out_ref, wide)

    return product_call(body, (own, others), windows, dtype, [])


def far_product(owns, place, other, near, near_place, windows, dtype):
    _, height, _ = other.shape
    stations = height // 2
    row, near_row = place * windows, near_place * windows

    def body(own_ref, other_ref, near_ref, out_ref, wide, twin):
        me = lax.axis_index("sta")
        end = jnp.logical_or(me == 0, me == lax.axis_size("sta") - 1)
        flags = own_ref[owns.shape[0] - 1, :8].astype(WIDE)
        alone = jnp.logical_and(end, jnp.max(flags) > 0.5)

        @pl.when(jnp.logical_not(alone))
        def _():
            unit(own_ref, row, other_ref, near_row, out_ref, wide)

        @pl.when(alone)
        def _():
            unit(own_ref, row, own_ref, row, twin.at[0], wide)
            unit(near_ref, near_row, near_ref, near_row, twin.at[1], wide)
            column = lax.broadcasted_iota(jnp.int32, (stations, LANES), 0)

            @pl.loop(0, stations)
            def _(a):
                one, two = twin[0, a], twin[1, a]
                re = jnp.where(column >= a, one[:stations], two[:stations])
                im = jnp.where(column >= a, one[stations:], two[stations:])
                im = jnp.where(column == a, two[:stations], im)
                out_ref[a, :stations] = re.astype(dtype)
                out_ref[a, stations:] = im.astype(dtype)

    twin = pltpu.VMEM((2, stations, height, LANES), WIDE)
    return product_call(body, (owns, other, near), windows, dtype, [twin])


def turn(a, value, buf_ref):
    height = value.shape[0]
    stations = height // 2
    for part in range(2):
        rows = value[part * stations : (part + 1) * stations]
        buf_ref[pl.ds(part * stations + a, stations, stride=height), :] = -rows if part else rows


def add_hours(parts, scale):
    shape = parts[0].shape
    stations, height, _ = shape

    def body(*refs):
        part_refs, (mine_ref, turned_ref, buf) = refs[: len(parts)], refs[len(parts) :]
        for a in range(stations):
            total = part_refs[0][a].astype(WIDE)
            for ref in part_refs[1:]:
                total = total + ref[a].astype(WIDE)
            total = total * scale
            mine_ref[a] = total
            turn(a, total, buf)
        for c in range(stations):
            turned_ref[c] = buf[pl.ds(c * height, height), :].astype(turned_ref.dtype)

    return pl.pallas_call(
        body,
        in_specs=[VMEM] * len(parts),
        out_specs=[VMEM] * 2,
        out_shape=[jax.ShapeDtypeStruct(shape, WIDE), jax.ShapeDtypeStruct(shape, jnp.bfloat16)],
        scratch_shapes=[pltpu.VMEM((stations * height, LANES), WIDE)],
        compiler_params=limits(4),
        name="add_hours",
    )(*parts)


def assemble(steps, near, far, turned):
    stations, height, _ = turned.shape
    pairs, tiles = steps.shape[0], 2

    def body(steps_ref, near_mine, near_theirs, far_mine, far_theirs, turned_ref, out_ref):
        first = near_tile()
        column = lax.broadcasted_iota(jnp.int32, (stations, LANES), 0)

        def put(p, a, tile, value):
            for part in range(2):
                rows = value[part * stations : (part + 1) * stations]
                out_ref[p, a, pl.ds(tile * 2 + part, stations, stride=2 * tiles), :] = rows

        def hermitian(p, a, tile, above, below, middle):
            re = jnp.where(column > a, above[:stations], below[:stations])
            im = jnp.where(column > a, above[stations:], below[stations:])
            re = jnp.where(column == a, middle, re)
            im = jnp.where(column == a, jnp.zeros_like(im), im)
            put(p, a, tile, jnp.concatenate([re, im], axis=0))

        for p in range(pairs):
            away = jnp.max(steps_ref[p])
            alone = jnp.abs(away) < 0.5
            inside = jnp.logical_and((away > 0.5) == (first == 1), jnp.logical_not(alone))
            outside = jnp.logical_not(jnp.logical_or(alone, inside))

            @pl.when(inside)
            def _(p=p):
                for a in range(stations):
                    put(p, a, first, near_mine[a])
                    put(p, a, 1 - first, near_theirs[a].astype(WIDE))

            @pl.when(outside)
            def _(p=p):
                for a in range(stations):
                    put(p, a, 1 - first, far_mine[a])
                    put(p, a, first, far_theirs[a].astype(WIDE))

            @pl.when(alone)
            def _(p=p):
                for a in range(stations):
                    own, back = far_mine[a], turned_ref[a].astype(WIDE)
                    hermitian(p, a, 1 - first, own, back, own[:stations])
                    hermitian(p, a, first, back, own, own[stations:])

    return pl.pallas_call(
        body,
        in_specs=[VMEM] * 6,
        out_specs=VMEM,
        out_shape=jax.ShapeDtypeStruct((pairs, stations, stations * tiles * 2, LANES), WIDE),
        compiler_params=limits(4),
        name="assemble",
    )(steps, *near, *far, turned)


def per_device(spectra, band_weight, station_order, pair_blocks):
    stations, _, windows, _, bins = spectra.shape
    tiles, pairs = bins // LANES, pair_blocks.shape[0]
    count, hours = lax.axis_size("sta"), lax.axis_size("hour")
    rows = spectra.reshape(stations, windows, 2, tiles, LANES)
    rows = rows.transpose(0, 1, 3, 2, 4).reshape(stations, windows, 2 * tiles, LANES)
    near, far, steps = whiten(rows, band_weight.reshape(tiles, LANES), station_order, pair_blocks, hours)

    on_chip = [(g, g ^ 1) for g in range(count)]
    across = [(g, h) for i in range(1, count - 1, 2) for g, h in ((i, i + 1), (i + 1, i))]

    def to_owner(part, d):
        return lax.ppermute(part, "hour", [(h, (h + d) % hours) for h in range(hours)]) if d else part

    def after(value, *earlier):
        return lax.optimization_barrier((value, earlier))[0]

    near_others = lax.ppermute(far, "sta", on_chip)
    far_others = [lax.ppermute(one, "sta", across) for one in near]
    dtypes = [jnp.bfloat16 if d else WIDE for d in ORDER]
    scale = 1.0 / (hours * windows)

    near_made = [
        near_product(near[k // BATCH], k % BATCH, near_others, k, windows, dtypes[k])
        for k in range(hours)
    ]
    near_parts = [to_owner(part, d) for part, d in zip(near_made, ORDER)]
    far_others[0] = after(far_others[0], *near_made)
    far_made = []
    for k in range(hours):
        batch, place = divmod(k, BATCH)
        if place == 0 and k:
            far_others[batch] = after(far_others[batch], *far_made)
        if k == 1:
            far_others[batch] = after(far_others[batch], near_parts[0], far_made[0])
        far_made.append(far_product(far, k, far_others[batch], near[batch], place, windows, dtypes[k]))
    far_parts = [to_owner(part, d) for part, d in zip(far_made, ORDER)]
    near_mine, turned = add_hours(after(near_parts[::-1], *far_made), scale)
    near_theirs = lax.ppermute(turned, "sta", on_chip)
    far_mine, turned = add_hours(after(far_parts[::-1], near_mine), scale)
    far_theirs = lax.ppermute(turned, "sta", across)
    cross = assemble(steps, (near_mine, near_theirs), (far_mine, far_theirs), turned)
    cross = cross.reshape(pairs, stations, stations, tiles // hours, 2, LANES)
    return cross.transpose(0, 1, 2, 4, 3, 5).reshape(pairs, stations, stations, 2, bins // hours)


def solution(mesh):
    return jax.shard_map(
        per_device,
        mesh=mesh,
        in_specs=(P("sta", "hour", None, None, None), P(), P("sta", None), P("sta", None)),
        out_specs=P("sta", None, None, None, "hour"),
        check_vma=False,
    )
```

```python
import jax
import jax.numpy as jnp
from jax import lax
from jax.experimental import pallas as pl
from jax.experimental.pallas import tpu as pltpu
from jax.sharding import PartitionSpec as P

LANES = 128
EPSILON = 1e-06
BLOCK = 8
ORDER = (2, 1, 3, 0)
BATCH = 2
WIDE = jnp.float32
VMEM = pl.BlockSpec(memory_space=pltpu.VMEM)


def limits(mib):
    return pltpu.CompilerParams(vmem_limit_bytes=mib << 20)


def near_tile():
    return 1 - lax.rem(lax.axis_index("sta"), 2)


def whiten(spectra, band_weight, station_order, pair_blocks, hours):
    stations, windows, rows, _ = spectra.shape
    tiles = rows // 2
    mine = tiles // hours
    chunks = 5
    step = windows // chunks
    batches = hours // BATCH
    height = 2 * stations

    def body(order_hbm, pairs_hbm, band_hbm, x_hbm, *refs):
        near_refs, (far_ref, steps_ref) = refs[:batches], refs[batches : batches + 2]
        order_ref, pairs_ref, band_ref, band, rowed, x_ref, sems, small = refs[batches + 2 :]

        def fetch(c):
            part = pl.ds(c * step, step)
            return pltpu.make_async_copy(x_hbm.at[:, part], x_ref.at[:, part], sems.at[c])

        fetch(0).start()
        copies = [
            pltpu.make_async_copy(order_hbm, order_ref, small.at[0]),
            pltpu.make_async_copy(pairs_hbm, pairs_ref, small.at[1]),
            pltpu.make_async_copy(band_hbm, band_ref, small.at[2]),
        ]
        for copy in copies:
            copy.start()
        for c in range(1, chunks):
            fetch(c).start()
        for copy in copies:
            copy.wait()
        for part in range(2):
            band[pl.ds(part, tiles, stride=2), :] = band_ref[...]
        weight = band[...]
        here, me, near = lax.axis_index("hour"), lax.axis_index("sta"), near_tile()
        asked = pairs_ref[0, 1] == me
        for p in range(pair_blocks.shape[0]):
            asked = jnp.logical_or(asked, pairs_ref[p, 1] == me)
            away = (pairs_ref[p, 1] - me).astype(WIDE)
            steps_ref[p] = jnp.full((8, LANES), away, WIDE)
        flag = jnp.where(asked, 1.0, 0.0)
        far_ref[hours * windows] = jnp.full((height, LANES), flag, WIDE).astype(jnp.bfloat16)

        @pl.loop(0, chunks)
        def _(c):
            fetch(c).wait()
            for w in range(step):
                for first in range(0, stations, BLOCK):
                    xs, squares = [], []
                    for k in range(BLOCK):
                        x = x_ref[order_ref[0, first + k], c * step + w].astype(WIDE)
                        xs.append(x)
                        squares.append(jnp.sum(x * x, axis=0, keepdims=True))
                    energy = jnp.sum(jnp.concatenate(squares, axis=0), axis=1, keepdims=True)
                    scale = lax.rsqrt(energy / (rows * LANES) + EPSILON)
                    scale = jnp.broadcast_to(scale, (BLOCK, LANES))
                    for k, x in enumerate(xs):
                        factor = jnp.broadcast_to(scale[k : k + 1], (rows, LANES))
                        place = pl.ds(w * rows * stations + first + k, rows, stride=stations)
                        rowed[place, :] = x * factor * weight
            for k, d in enumerate(ORDER):
                owner = lax.rem(here + d, hours)
                for w in range(step):
                    for tile, out, row in ((near, near_refs[k // BATCH], k % BATCH), (1 - near, far_ref, k)):
                        start = (w * tiles + owner * mine + tile) * height
                        white = rowed[pl.ds(pl.multiple_of(start, height), height), :]
                        out[row * windows + c * step + w] = white.astype(jnp.bfloat16)

    hbm = pl.BlockSpec(memory_space=pltpu.HBM)
    inputs = (station_order, pair_blocks, band_weight, spectra)
    outs = pl.pallas_call(
        body,
        in_specs=[hbm] * 4,
        out_specs=[VMEM] * (batches + 2),
        out_shape=[jax.ShapeDtypeStruct((BATCH * windows, height, LANES), jnp.bfloat16)] * batches
        + [
            jax.ShapeDtypeStruct((hours * windows + 1, height, LANES), jnp.bfloat16),
            jax.ShapeDtypeStruct((pair_blocks.shape[0], 8, LANES), WIDE),
        ],
        scratch_shapes=[
            pltpu.SMEM(station_order.shape, jnp.int32),
            pltpu.SMEM(pair_blocks.shape, jnp.int32),
            pltpu.VMEM((tiles, LANES), WIDE),
            pltpu.VMEM((rows, LANES), WIDE),
            pltpu.VMEM((step * rows * stations, LANES), WIDE),
            pltpu.VMEM(spectra.shape, jnp.bfloat16),
            pltpu.SemaphoreType.DMA((chunks,)),
            pltpu.SemaphoreType.DMA((3,)),
        ],
        compiler_params=limits(8),
        name="whiten",
    )(*[pltpu.with_memory_space_constraint(value, pltpu.HBM) for value in inputs])
    return outs[:batches], outs[batches], outs[batches + 1]


def unit(own_ref, own_row, other_ref, other_row, out_ref, wide):
    stations = own_ref.shape[1] // 2
    windows = wide.shape[0]
    wide[...] = own_ref[pl.ds(own_row, windows)].astype(WIDE)
    for first in range(0, stations, BLOCK):

        def body(w, sums):
            other = other_ref[other_row + w].astype(WIDE)
            re, im = other[:stations], other[stations:]
            new = []
            for k in range(BLOCK):
                a = first + k
                a_re = jnp.broadcast_to(wide[w, a : a + 1, :], re.shape)
                a_im = jnp.broadcast_to(wide[w, stations + a : stations + a + 1, :], re.shape)
                new.append(sums[2 * k] + (a_re * re + a_im * im))
                new.append(sums[2 * k + 1] + (a_re * im - a_im * re))
            return tuple(new)

        zero = jnp.zeros((stations, LANES), WIDE)
        sums = lax.fori_loop(0, windows, body, (zero,) * (2 * BLOCK), unroll=6)
        for k in range(BLOCK):
            out_ref[first + k, :stations] = sums[2 * k].astype(out_ref.dtype)
            out_ref[first + k, stations:] = sums[2 * k + 1].astype(out_ref.dtype)


def product_call(body, operands, windows, dtype, scratch_shapes):
    height = operands[0].shape[1]
    stations = height // 2
    return pl.pallas_call(
        body,
        in_specs=[VMEM] * len(operands),
        out_specs=VMEM,
        out_shape=jax.ShapeDtypeStruct((stations, height, LANES), dtype),
        scratch_shapes=[pltpu.VMEM((windows, height, LANES), WIDE)] + scratch_shapes,
        compiler_params=limits(4),
        cost_estimate=pl.CostEstimate(
            flops=stations * stations * LANES * windows * 8, bytes_accessed=1 << 19, transcendentals=0
        ),
        name="products",
    )(*operands)


def near_product(own, own_place, others, place, windows, dtype):
    def body(own_ref, other_ref, out_ref, wide):
        unit(own_ref, own_place * windows, other_ref, place * windows, out_ref, wide)

    return product_call(body, (own, others), windows, dtype, [])


def far_product(owns, place, other, near, near_place, windows, dtype):
    _, height, _ = other.shape
    stations = height // 2
    row, near_row = place * windows, near_place * windows

    def body(own_ref, other_ref, near_ref, out_ref, wide, twin):
        me = lax.axis_index("sta")
        end = jnp.logical_or(me == 0, me == lax.axis_size("sta") - 1)
        flags = own_ref[owns.shape[0] - 1, :8].astype(WIDE)
        alone = jnp.logical_and(end, jnp.max(flags) > 0.5)

        @pl.when(jnp.logical_not(alone))
        def _():
            unit(own_ref, row, other_ref, near_row, out_ref, wide)

        @pl.when(alone)
        def _():
            unit(own_ref, row, own_ref, row, twin.at[0], wide)
            unit(near_ref, near_row, near_ref, near_row, twin.at[1], wide)
            column = lax.broadcasted_iota(jnp.int32, (stations, LANES), 0)

            @pl.loop(0, stations)
            def _(a):
                one, two = twin[0, a], twin[1, a]
                re = jnp.where(column >= a, one[:stations], two[:stations])
                im = jnp.where(column >= a, one[stations:], two[stations:])
                im = jnp.where(column == a, two[:stations], im)
                out_ref[a, :stations] = re.astype(dtype)
                out_ref[a, stations:] = im.astype(dtype)

    twin = pltpu.VMEM((2, stations, height, LANES), WIDE)
    return product_call(body, (owns, other, near), windows, dtype, [twin])


def turn(a, value, buf_ref):
    height = value.shape[0]
    stations = height // 2
    for part in range(2):
        rows = value[part * stations : (part + 1) * stations]
        buf_ref[pl.ds(part * stations + a, stations, stride=height), :] = -rows if part else rows


def add_hours(parts, scale):
    shape = parts[0].shape
    stations, height, _ = shape

    def body(*refs):
        part_refs, (mine_ref, turned_ref, buf) = refs[: len(parts)], refs[len(parts) :]
        for a in range(stations):
            total = part_refs[0][a].astype(WIDE)
            for ref in part_refs[1:]:
                total = total + ref[a].astype(WIDE)
            total = total * scale
            mine_ref[a] = total
            turn(a, total, buf)
        for c in range(stations):
            turned_ref[c] = buf[pl.ds(c * height, height), :].astype(turned_ref.dtype)

    return pl.pallas_call(
        body,
        in_specs=[VMEM] * len(parts),
        out_specs=[VMEM] * 2,
        out_shape=[jax.ShapeDtypeStruct(shape, WIDE), jax.ShapeDtypeStruct(shape, jnp.bfloat16)],
        scratch_shapes=[pltpu.VMEM((stations * height, LANES), WIDE)],
        compiler_params=limits(4),
        name="add_hours",
    )(*parts)


def assemble(steps, near, far, turned):
    stations, height, _ = turned.shape
    pairs, tiles = steps.shape[0], 2

    def body(steps_ref, near_mine, near_theirs, far_mine, far_theirs, turned_ref, out_ref):
        first = near_tile()
        column = lax.broadcasted_iota(jnp.int32, (stations, LANES), 0)

        def put(p, a, tile, value):
            for part in range(2):
                rows = value[part * stations : (part + 1) * stations]
                out_ref[p, a, pl.ds(tile * 2 + part, stations, stride=2 * tiles), :] = rows

        def hermitian(p, a, tile, above, below, middle):
            re = jnp.where(column > a, above[:stations], below[:stations])
            im = jnp.where(column > a, above[stations:], below[stations:])
            re = jnp.where(column == a, middle, re)
            im = jnp.where(column == a, jnp.zeros_like(im), im)
            put(p, a, tile, jnp.concatenate([re, im], axis=0))

        for p in range(pairs):
            away = jnp.max(steps_ref[p])
            alone = jnp.abs(away) < 0.5
            inside = jnp.logical_and((away > 0.5) == (first == 1), jnp.logical_not(alone))
            outside = jnp.logical_not(jnp.logical_or(alone, inside))

            @pl.when(inside)
            def _(p=p):
                for a in range(stations):
                    put(p, a, first, near_mine[a])
                    put(p, a, 1 - first, near_theirs[a].astype(WIDE))

            @pl.when(outside)
            def _(p=p):
                for a in range(stations):
                    put(p, a, 1 - first, far_mine[a])
                    put(p, a, first, far_theirs[a].astype(WIDE))

            @pl.when(alone)
            def _(p=p):
                for a in range(stations):
                    own, back = far_mine[a], turned_ref[a].astype(WIDE)
                    hermitian(p, a, 1 - first, own, back, own[:stations])
                    hermitian(p, a, first, back, own, own[stations:])

    return pl.pallas_call(
        body,
        in_specs=[VMEM] * 6,
        out_specs=VMEM,
        out_shape=jax.ShapeDtypeStruct((pairs, stations, stations * tiles * 2, LANES), WIDE),
        compiler_params=limits(4),
        name="assemble",
    )(steps, *near, *far, turned)


def per_device(spectra, band_weight, station_order, pair_blocks):
    stations, _, windows, _, bins = spectra.shape
    tiles, pairs = bins // LANES, pair_blocks.shape[0]
    count, hours = lax.axis_size("sta"), lax.axis_size("hour")
    rows = spectra.reshape(stations, windows, 2, tiles, LANES)
    rows = rows.transpose(0, 1, 3, 2, 4).reshape(stations, windows, 2 * tiles, LANES)
    near, far, steps = whiten(rows, band_weight.reshape(tiles, LANES), station_order, pair_blocks, hours)

    on_chip = [(g, g ^ 1) for g in range(count)]
    across = [(g, h) for i in range(1, count - 1, 2) for g, h in ((i, i + 1), (i + 1, i))]

    def to_owner(part, d):
        return lax.ppermute(part, "hour", [(h, (h + d) % hours) for h in range(hours)]) if d else part

    def after(value, *earlier):
        return lax.optimization_barrier((value, earlier))[0]

    near_others = lax.ppermute(far, "sta", on_chip)
    far_others = [lax.ppermute(near[0], "sta", across)]
    dtypes = [jnp.bfloat16 if d else WIDE for d in ORDER]
    scale = 1.0 / (hours * windows)

    near_made = [
        near_product(near[k // BATCH], k % BATCH, near_others, k, windows, dtypes[k])
        for k in range(hours)
    ]
    far_others.append(lax.ppermute(after(near[1], *near_made[:1]), "sta", across))
    near_parts = [to_owner(part, d) for part, d in zip(near_made, ORDER)]
    far_others[0] = after(far_others[0], *near_made)
    far_made = []
    for k in range(hours):
        batch, place = divmod(k, BATCH)
        if place == 0 and k:
            far_others[batch] = after(far_others[batch], *far_made)
        if k == 1:
            far_others[batch] = after(far_others[batch], near_parts[0], far_made[0])
        far_made.append(far_product(far, k, far_others[batch], near[batch], place, windows, dtypes[k]))
    far_parts = [to_owner(part, d) for part, d in zip(far_made, ORDER)]
    near_mine, turned = add_hours(after(near_parts[::-1], *far_made), scale)
    near_theirs = lax.ppermute(turned, "sta", on_chip)
    far_mine, turned = add_hours(after(far_parts[::-1], near_mine), scale)
    far_theirs = lax.ppermute(turned, "sta", across)
    cross = assemble(steps, (near_mine, near_theirs), (far_mine, far_theirs), turned)
    cross = cross.reshape(pairs, stations, stations, tiles // hours, 2, LANES)
    return cross.transpose(0, 1, 2, 4, 3, 5).reshape(pairs, stations, stations, 2, bins // hours)


def solution(mesh):
    return jax.shard_map(
        per_device,
        mesh=mesh,
        in_specs=(P("sta", "hour", None, None, None), P(), P("sta", None), P("sta", None)),
        out_specs=P("sta", None, None, None, "hour"),
        check_vma=False,
    )
```

```python
import jax
import jax.numpy as jnp
from jax import lax
from jax.experimental import pallas as pl
from jax.experimental.pallas import tpu as pltpu
from jax.sharding import PartitionSpec as P

LANES = 128
EPSILON = 1e-06
BLOCK = 8
ORDER = (2, 3, 1, 0)
BATCH = 2
WIDE = jnp.float32
VMEM = pl.BlockSpec(memory_space=pltpu.VMEM)


def limits(mib):
    return pltpu.CompilerParams(vmem_limit_bytes=mib << 20)


def near_tile():
    return 1 - lax.rem(lax.axis_index("sta"), 2)


def whiten(spectra, band_weight, station_order, pair_blocks, hours):
    stations, windows, rows, _ = spectra.shape
    tiles = rows // 2
    mine = tiles // hours
    chunks = 5
    step = windows // chunks
    batches = hours // BATCH
    height = 2 * stations

    def body(order_hbm, pairs_hbm, band_hbm, x_hbm, *refs):
        near_refs, (far_ref, steps_ref) = refs[:batches], refs[batches : batches + 2]
        order_ref, pairs_ref, band_ref, band, rowed, x_ref, sems, small = refs[batches + 2 :]

        def fetch(c):
            part = pl.ds(c * step, step)
            return pltpu.make_async_copy(x_hbm.at[:, part], x_ref.at[:, part], sems.at[c])

        fetch(0).start()
        copies = [
            pltpu.make_async_copy(order_hbm, order_ref, small.at[0]),
            pltpu.make_async_copy(pairs_hbm, pairs_ref, small.at[1]),
            pltpu.make_async_copy(band_hbm, band_ref, small.at[2]),
        ]
        for copy in copies:
            copy.start()
        for c in range(1, chunks):
            fetch(c).start()
        for copy in copies:
            copy.wait()
        for part in range(2):
            band[pl.ds(part, tiles, stride=2), :] = band_ref[...]
        weight = band[...]
        here, me, near = lax.axis_index("hour"), lax.axis_index("sta"), near_tile()
        asked = pairs_ref[0, 1] == me
        for p in range(pair_blocks.shape[0]):
            asked = jnp.logical_or(asked, pairs_ref[p, 1] == me)
            away = (pairs_ref[p, 1] - me).astype(WIDE)
            steps_ref[p] = jnp.full((8, LANES), away, WIDE)
        flag = jnp.where(asked, 1.0, 0.0)
        far_ref[hours * windows] = jnp.full((height, LANES), flag, WIDE).astype(jnp.bfloat16)

        @pl.loop(0, chunks)
        def _(c):
            fetch(c).wait()
            for w in range(step):
                for first in range(0, stations, BLOCK):
                    xs, squares = [], []
                    for k in range(BLOCK):
                        x = x_ref[order_ref[0, first + k], c * step + w].astype(WIDE)
                        xs.append(x)
                        squares.append(jnp.sum(x * x, axis=0, keepdims=True))
                    energy = jnp.sum(jnp.concatenate(squares, axis=0), axis=1, keepdims=True)
                    scale = lax.rsqrt(energy / (rows * LANES) + EPSILON)
                    scale = jnp.broadcast_to(scale, (BLOCK, LANES))
                    for k, x in enumerate(xs):
                        factor = jnp.broadcast_to(scale[k : k + 1], (rows, LANES))
                        place = pl.ds(w * rows * stations + first + k, rows, stride=stations)
                        rowed[place, :] = x * factor * weight
            for k, d in enumerate(ORDER):
                owner = lax.bitwise_xor(here, d)
                for w in range(step):
                    for tile, out, row in ((near, near_refs[k // BATCH], k % BATCH), (1 - near, far_ref, k)):
                        start = (w * tiles + owner * mine + tile) * height
                        white = rowed[pl.ds(pl.multiple_of(start, height), height), :]
                        out[row * windows + c * step + w] = white.astype(jnp.bfloat16)

    hbm = pl.BlockSpec(memory_space=pltpu.HBM)
    inputs = (station_order, pair_blocks, band_weight, spectra)
    outs = pl.pallas_call(
        body,
        in_specs=[hbm] * 4,
        out_specs=[VMEM] * (batches + 2),
        out_shape=[jax.ShapeDtypeStruct((BATCH * windows, height, LANES), jnp.bfloat16)] * batches
        + [
            jax.ShapeDtypeStruct((hours * windows + 1, height, LANES), jnp.bfloat16),
            jax.ShapeDtypeStruct((pair_blocks.shape[0], 8, LANES), WIDE),
        ],
        scratch_shapes=[
            pltpu.SMEM(station_order.shape, jnp.int32),
            pltpu.SMEM(pair_blocks.shape, jnp.int32),
            pltpu.VMEM((tiles, LANES), WIDE),
            pltpu.VMEM((rows, LANES), WIDE),
            pltpu.VMEM((step * rows * stations, LANES), WIDE),
            pltpu.VMEM(spectra.shape, jnp.bfloat16),
            pltpu.SemaphoreType.DMA((chunks,)),
            pltpu.SemaphoreType.DMA((3,)),
        ],
        compiler_params=limits(8),
        name="whiten",
    )(*[pltpu.with_memory_space_constraint(value, pltpu.HBM) for value in inputs])
    return outs[:batches], outs[batches], outs[batches + 1]


def unit(own_ref, own_row, other_ref, other_row, out_ref, wide):
    stations = own_ref.shape[1] // 2
    windows, block = wide.shape[0], 4
    wide[...] = own_ref[pl.ds(own_row, windows)].astype(WIDE)
    for first in range(0, stations, block):

        def body(w, sums):
            other = other_ref[other_row + w].astype(WIDE)
            re, im = other[:stations], other[stations:]
            gap = im - re
            new = []
            for k in range(block):
                a = first + k
                a_re = jnp.broadcast_to(wide[w, a : a + 1, :], re.shape)
                a_im = jnp.broadcast_to(wide[w, stations + a : stations + a + 1, :], re.shape)
                p, q, r = sums[3 * k : 3 * k + 3]
                new += [p + a_re * re, q + a_im * im, r + (a_re + a_im) * gap]
            return tuple(new)

        zero = jnp.zeros((stations, LANES), WIDE)
        sums = lax.fori_loop(0, windows, body, (zero,) * (3 * block), unroll=windows)
        for k in range(block):
            p, q, r = sums[3 * k : 3 * k + 3]
            out_ref[first + k, :stations] = (p + q).astype(out_ref.dtype)
            out_ref[first + k, stations:] = (r + p - q).astype(out_ref.dtype)


def product_call(body, operands, windows, dtype, scratch_shapes):
    height = operands[0].shape[1]
    stations = height // 2
    return pl.pallas_call(
        body,
        in_specs=[VMEM] * len(operands),
        out_specs=VMEM,
        out_shape=jax.ShapeDtypeStruct((stations, height, LANES), dtype),
        scratch_shapes=[pltpu.VMEM((windows, height, LANES), WIDE)] + scratch_shapes,
        compiler_params=limits(4),
        cost_estimate=pl.CostEstimate(
            flops=stations * stations * LANES * windows * 8, bytes_accessed=1 << 19, transcendentals=0
        ),
        name="products",
    )(*operands)


def near_product(own, own_place, others, place, windows, dtype):
    def body(own_ref, other_ref, out_ref, wide):
        unit(own_ref, own_place * windows, other_ref, place * windows, out_ref, wide)

    return product_call(body, (own, others), windows, dtype, [])


def far_product(owns, place, other, near, near_place, windows, dtype):
    _, height, _ = other.shape
    stations = height // 2
    row, near_row = place * windows, near_place * windows

    def body(own_ref, other_ref, near_ref, out_ref, wide, twin):
        me = lax.axis_index("sta")
        end = jnp.logical_or(me == 0, me == lax.axis_size("sta") - 1)
        flags = own_ref[owns.shape[0] - 1, :8].astype(WIDE)
        alone = jnp.logical_and(end, jnp.max(flags) > 0.5)

        @pl.when(jnp.logical_not(alone))
        def _():
            unit(own_ref, row, other_ref, near_row, out_ref, wide)

        @pl.when(alone)
        def _():
            unit(own_ref, row, own_ref, row, twin.at[0], wide)
            unit(near_ref, near_row, near_ref, near_row, twin.at[1], wide)
            column = lax.broadcasted_iota(jnp.int32, (stations, LANES), 0)

            @pl.loop(0, stations)
            def _(a):
                one, two = twin[0, a], twin[1, a]
                re = jnp.where(column >= a, one[:stations], two[:stations])
                im = jnp.where(column >= a, one[stations:], two[stations:])
                im = jnp.where(column == a, two[:stations], im)
                out_ref[a, :stations] = re.astype(dtype)
                out_ref[a, stations:] = im.astype(dtype)

    twin = pltpu.VMEM((2, stations, height, LANES), WIDE)
    return product_call(body, (owns, other, near), windows, dtype, [twin])


def turn(a, value, buf_ref):
    height = value.shape[0]
    stations = height // 2
    for part in range(2):
        rows = value[part * stations : (part + 1) * stations]
        buf_ref[pl.ds(part * stations + a, stations, stride=height), :] = -rows if part else rows


def add_hours(parts, scale):
    shape = parts[0].shape
    stations, height, _ = shape

    def body(*refs):
        part_refs, (mine_ref, turned_ref, buf) = refs[: len(parts)], refs[len(parts) :]
        for a in range(stations):
            total = part_refs[0][a].astype(WIDE)
            for ref in part_refs[1:]:
                total = total + ref[a].astype(WIDE)
            total = total * scale
            mine_ref[a] = total
            turn(a, total, buf)
        for c in range(stations):
            turned_ref[c] = buf[pl.ds(c * height, height), :].astype(turned_ref.dtype)

    return pl.pallas_call(
        body,
        in_specs=[VMEM] * len(parts),
        out_specs=[VMEM] * 2,
        out_shape=[jax.ShapeDtypeStruct(shape, WIDE), jax.ShapeDtypeStruct(shape, jnp.bfloat16)],
        scratch_shapes=[pltpu.VMEM((stations * height, LANES), WIDE)],
        compiler_params=limits(4),
        name="add_hours",
    )(*parts)


def assemble(steps, near, far, turned):
    stations, height, _ = turned.shape
    pairs, tiles = steps.shape[0], 2

    def body(steps_ref, near_mine, near_theirs, far_mine, far_theirs, turned_ref, out_ref):
        first = near_tile()
        column = lax.broadcasted_iota(jnp.int32, (stations, LANES), 0)

        def put(p, a, tile, value):
            for part in range(2):
                rows = value[part * stations : (part + 1) * stations]
                out_ref[p, a, pl.ds(tile * 2 + part, stations, stride=2 * tiles), :] = rows

        def hermitian(p, a, tile, above, below, middle):
            re = jnp.where(column > a, above[:stations], below[:stations])
            im = jnp.where(column > a, above[stations:], below[stations:])
            re = jnp.where(column == a, middle, re)
            im = jnp.where(column == a, jnp.zeros_like(im), im)
            put(p, a, tile, jnp.concatenate([re, im], axis=0))

        for p in range(pairs):
            away = jnp.max(steps_ref[p])
            alone = jnp.abs(away) < 0.5
            inside = jnp.logical_and((away > 0.5) == (first == 1), jnp.logical_not(alone))
            outside = jnp.logical_not(jnp.logical_or(alone, inside))

            @pl.when(inside)
            def _(p=p):
                for a in range(stations):
                    put(p, a, first, near_mine[a])
                    put(p, a, 1 - first, near_theirs[a].astype(WIDE))

            @pl.when(outside)
            def _(p=p):
                for a in range(stations):
                    put(p, a, 1 - first, far_mine[a])
                    put(p, a, first, far_theirs[a].astype(WIDE))

            @pl.when(alone)
            def _(p=p):
                for a in range(stations):
                    own, back = far_mine[a], turned_ref[a].astype(WIDE)
                    hermitian(p, a, 1 - first, own, back, own[:stations])
                    hermitian(p, a, first, back, own, own[stations:])

    return pl.pallas_call(
        body,
        in_specs=[VMEM] * 6,
        out_specs=VMEM,
        out_shape=jax.ShapeDtypeStruct((pairs, stations, stations * tiles * 2, LANES), WIDE),
        compiler_params=limits(4),
        name="assemble",
    )(steps, *near, *far, turned)


def per_device(spectra, band_weight, station_order, pair_blocks):
    stations, _, windows, _, bins = spectra.shape
    tiles, pairs = bins // LANES, pair_blocks.shape[0]
    count, hours = lax.axis_size("sta"), lax.axis_size("hour")
    rows = spectra.reshape(stations, windows, 2, tiles, LANES)
    rows = rows.transpose(0, 1, 3, 2, 4).reshape(stations, windows, 2 * tiles, LANES)
    near, far, steps = whiten(rows, band_weight.reshape(tiles, LANES), station_order, pair_blocks, hours)

    on_chip = [(g, g ^ 1) for g in range(count)]
    across = [(g, h) for i in range(1, count - 1, 2) for g, h in ((i, i + 1), (i + 1, i))]

    def to_owner(part, d):
        return lax.ppermute(part, "hour", [(h, h ^ d) for h in range(hours)]) if d else part

    def after(value, *earlier):
        return lax.optimization_barrier((value, earlier))[0]

    near_others = lax.ppermute(far, "sta", on_chip)
    far_others = [lax.ppermute(near[0], "sta", across)]
    dtypes = [jnp.bfloat16 if d else WIDE for d in ORDER]
    scale = 1.0 / (hours * windows)

    near_made = [
        near_product(near[k // BATCH], k % BATCH, near_others, k, windows, dtypes[k])
        for k in range(hours)
    ]
    far_others.append(lax.ppermute(after(near[1], *near_made[:1]), "sta", across))
    near_parts = [to_owner(part, d) for part, d in zip(near_made, ORDER)]
    far_others[0] = after(far_others[0], *near_made)
    far_made = []
    for k in range(hours):
        batch, place = divmod(k, BATCH)
        if place == 0 and k:
            far_others[batch] = after(far_others[batch], *far_made)
        if k == 1:
            far_others[batch] = after(far_others[batch], near_parts[0], far_made[0])
        far_made.append(far_product(far, k, far_others[batch], near[batch], place, windows, dtypes[k]))
    far_parts = [to_owner(part, d) for part, d in zip(far_made, ORDER)]
    near_mine, turned = add_hours(after(near_parts[::-1], *far_made), scale)
    near_theirs = lax.ppermute(turned, "sta", on_chip)
    far_mine, turned = add_hours(after(far_parts[::-1], near_mine), scale)
    far_theirs = lax.ppermute(turned, "sta", across)
    cross = assemble(steps, (near_mine, near_theirs), (far_mine, far_theirs), turned)
    cross = cross.reshape(pairs, stations, stations, tiles // hours, 2, LANES)
    return cross.transpose(0, 1, 2, 4, 3, 5).reshape(pairs, stations, stations, 2, bins // hours)


def solution(mesh):
    return jax.shard_map(
        per_device,
        mesh=mesh,
        in_specs=(P("sta", "hour", None, None, None), P(), P("sta", None), P("sta", None)),
        out_specs=P("sta", None, None, None, "hour"),
        check_vma=False,
    )
```

```python
import jax
import jax.numpy as jnp
from jax import lax
from jax.experimental import pallas as pl
from jax.experimental.pallas import tpu as pltpu
from jax.sharding import PartitionSpec as P

LANES = 128
EPSILON = 1e-06
BLOCK = 8
ORDER = (2, 3, 1, 0)
BATCH = 2
WIDE = jnp.float32
VMEM = pl.BlockSpec(memory_space=pltpu.VMEM)


def limits(mib):
    return pltpu.CompilerParams(vmem_limit_bytes=mib << 20)


def near_tile():
    return 1 - lax.rem(lax.axis_index("sta"), 2)


def whiten(spectra, band_weight, station_order, pair_blocks, hours):
    stations, windows, rows, _ = spectra.shape
    tiles = rows // 2
    mine = tiles // hours
    chunks = 5
    step = windows // chunks
    batches = hours // BATCH
    height = 2 * stations

    def body(order_hbm, pairs_hbm, band_hbm, x_hbm, *refs):
        near_refs, (far_ref, steps_ref) = refs[:batches], refs[batches : batches + 2]
        order_ref, pairs_ref, band_ref, band, rowed, x_ref, sems, small = refs[batches + 2 :]

        def fetch(c):
            part = pl.ds(c * step, step)
            return pltpu.make_async_copy(x_hbm.at[:, part], x_ref.at[:, part], sems.at[c])

        fetch(0).start()
        copies = [
            pltpu.make_async_copy(order_hbm, order_ref, small.at[0]),
            pltpu.make_async_copy(pairs_hbm, pairs_ref, small.at[1]),
            pltpu.make_async_copy(band_hbm, band_ref, small.at[2]),
        ]
        for copy in copies:
            copy.start()
        for c in range(1, chunks):
            fetch(c).start()
        for copy in copies:
            copy.wait()
        for part in range(2):
            band[pl.ds(part, tiles, stride=2), :] = band_ref[...]
        weight = band[...]
        here, me, near = lax.axis_index("hour"), lax.axis_index("sta"), near_tile()
        asked = pairs_ref[0, 1] == me
        for p in range(pair_blocks.shape[0]):
            asked = jnp.logical_or(asked, pairs_ref[p, 1] == me)
            away = (pairs_ref[p, 1] - me).astype(WIDE)
            steps_ref[p] = jnp.full((8, LANES), away, WIDE)
        flag = jnp.where(asked, 1.0, 0.0)
        far_ref[hours * windows] = jnp.full((height, LANES), flag, WIDE).astype(jnp.bfloat16)

        @pl.loop(0, chunks)
        def _(c):
            fetch(c).wait()
            for w in range(step):
                for first in range(0, stations, BLOCK):
                    xs, squares = [], []
                    for k in range(BLOCK):
                        x = x_ref[order_ref[0, first + k], c * step + w].astype(WIDE)
                        xs.append(x)
                        squares.append(jnp.sum(x * x, axis=0, keepdims=True))
                    energy = jnp.sum(jnp.concatenate(squares, axis=0), axis=1, keepdims=True)
                    scale = lax.rsqrt(energy / (rows * LANES) + EPSILON)
                    scale = jnp.broadcast_to(scale, (BLOCK, LANES))
                    for k, x in enumerate(xs):
                        factor = jnp.broadcast_to(scale[k : k + 1], (rows, LANES))
                        place = pl.ds(w * rows * stations + first + k, rows, stride=stations)
                        rowed[place, :] = x * factor * weight
            for k, d in enumerate(ORDER):
                owner = lax.bitwise_xor(here, d)
                for w in range(step):
                    for tile, out, row in ((near, near_refs[k // BATCH], k % BATCH), (1 - near, far_ref, k)):
                        start = (w * tiles + owner * mine + tile) * height
                        white = rowed[pl.ds(pl.multiple_of(start, height), height), :]
                        out[row * windows + c * step + w] = white.astype(jnp.bfloat16)

    hbm = pl.BlockSpec(memory_space=pltpu.HBM)
    inputs = (station_order, pair_blocks, band_weight, spectra)
    outs = pl.pallas_call(
        body,
        in_specs=[hbm] * 4,
        out_specs=[VMEM] * (batches + 2),
        out_shape=[jax.ShapeDtypeStruct((BATCH * windows, height, LANES), jnp.bfloat16)] * batches
        + [
            jax.ShapeDtypeStruct((hours * windows + 1, height, LANES), jnp.bfloat16),
            jax.ShapeDtypeStruct((pair_blocks.shape[0], 8, LANES), WIDE),
        ],
        scratch_shapes=[
            pltpu.SMEM(station_order.shape, jnp.int32),
            pltpu.SMEM(pair_blocks.shape, jnp.int32),
            pltpu.VMEM((tiles, LANES), WIDE),
            pltpu.VMEM((rows, LANES), WIDE),
            pltpu.VMEM((step * rows * stations, LANES), WIDE),
            pltpu.VMEM(spectra.shape, jnp.bfloat16),
            pltpu.SemaphoreType.DMA((chunks,)),
            pltpu.SemaphoreType.DMA((3,)),
        ],
        compiler_params=limits(8),
        name="whiten",
    )(*[pltpu.with_memory_space_constraint(value, pltpu.HBM) for value in inputs])
    return outs[:batches], outs[batches], outs[batches + 1]


def unit(own_ref, own_row, other_ref, other_row, out_ref, wide):
    stations = own_ref.shape[1] // 2
    windows, block = wide.shape[0], 4
    wide[...] = own_ref[pl.ds(own_row, windows)].astype(WIDE)
    for first in range(0, stations, block):

        def body(w, sums):
            other = other_ref[other_row + w].astype(WIDE)
            re, im = other[:stations], other[stations:]
            gap = im - re
            new = []
            for k in range(block):
                a = first + k
                a_re = jnp.broadcast_to(wide[w, a : a + 1, :], re.shape)
                a_im = jnp.broadcast_to(wide[w, stations + a : stations + a + 1, :], re.shape)
                p, q, r = sums[3 * k : 3 * k + 3]
                new += [p + a_re * re, q + a_im * im, r + (a_re + a_im) * gap]
            return tuple(new)

        zero = jnp.zeros((stations, LANES), WIDE)
        sums = lax.fori_loop(0, windows, body, (zero,) * (3 * block), unroll=windows)
        for k in range(block):
            p, q, r = sums[3 * k : 3 * k + 3]
            out_ref[first + k, :stations] = (p + q).astype(out_ref.dtype)
            out_ref[first + k, stations:] = (r + p - q).astype(out_ref.dtype)


def product_call(body, operands, windows, dtype, scratch_shapes):
    height = operands[0].shape[1]
    stations = height // 2
    return pl.pallas_call(
        body,
        in_specs=[VMEM] * len(operands),
        out_specs=VMEM,
        out_shape=jax.ShapeDtypeStruct((stations, height, LANES), dtype),
        scratch_shapes=[pltpu.VMEM((windows, height, LANES), WIDE)] + scratch_shapes,
        compiler_params=limits(4),
        cost_estimate=pl.CostEstimate(
            flops=stations * stations * LANES * windows * 8, bytes_accessed=1 << 19, transcendentals=0
        ),
        name="products",
    )(*operands)


def near_product(own, own_place, others, place, windows, dtype):
    def body(own_ref, other_ref, out_ref, wide):
        unit(own_ref, own_place * windows, other_ref, place * windows, out_ref, wide)

    return product_call(body, (own, others), windows, dtype, [])


def far_product(owns, place, other, near, near_place, windows, dtype):
    _, height, _ = other.shape
    stations = height // 2
    row, near_row = place * windows, near_place * windows

    def body(own_ref, other_ref, near_ref, out_ref, wide, twin):
        me = lax.axis_index("sta")
        end = jnp.logical_or(me == 0, me == lax.axis_size("sta") - 1)
        flags = own_ref[owns.shape[0] - 1, :8].astype(WIDE)
        alone = jnp.logical_and(end, jnp.max(flags) > 0.5)

        @pl.when(jnp.logical_not(alone))
        def _():
            unit(own_ref, row, other_ref, near_row, out_ref, wide)

        @pl.when(alone)
        def _():
            unit(own_ref, row, own_ref, row, twin.at[0], wide)
            unit(near_ref, near_row, near_ref, near_row, twin.at[1], wide)
            column = lax.broadcasted_iota(jnp.int32, (stations, LANES), 0)

            @pl.loop(0, stations)
            def _(a):
                one, two = twin[0, a], twin[1, a]
                re = jnp.where(column >= a, one[:stations], two[:stations])
                im = jnp.where(column >= a, one[stations:], two[stations:])
                im = jnp.where(column == a, two[:stations], im)
                out_ref[a, :stations] = re.astype(dtype)
                out_ref[a, stations:] = im.astype(dtype)

    twin = pltpu.VMEM((2, stations, height, LANES), WIDE)
    return product_call(body, (owns, other, near), windows, dtype, [twin])


def turn(a, value, buf_ref):
    height = value.shape[0]
    stations = height // 2
    for part in range(2):
        rows = value[part * stations : (part + 1) * stations]
        buf_ref[pl.ds(part * stations + a, stations, stride=height), :] = -rows if part else rows


def add_hours(parts, scale):
    shape = parts[0].shape
    stations, height, _ = shape

    def body(*refs):
        part_refs, (mine_ref, turned_ref, buf) = refs[: len(parts)], refs[len(parts) :]
        for a in range(stations):
            total = part_refs[0][a].astype(WIDE)
            for ref in part_refs[1:]:
                total = total + ref[a].astype(WIDE)
            total = total * scale
            mine_ref[a] = total
            turn(a, total, buf)
        for c in range(stations):
            turned_ref[c] = buf[pl.ds(c * height, height), :].astype(turned_ref.dtype)

    return pl.pallas_call(
        body,
        in_specs=[VMEM] * len(parts),
        out_specs=[VMEM] * 2,
        out_shape=[jax.ShapeDtypeStruct(shape, WIDE), jax.ShapeDtypeStruct(shape, jnp.bfloat16)],
        scratch_shapes=[pltpu.VMEM((stations * height, LANES), WIDE)],
        compiler_params=limits(4),
        name="add_hours",
    )(*parts)


def assemble(steps, near, far=None, turned=None, done=None):
    operands = (steps, *near) if done is None else (done, steps, *far, turned)
    stations, height, _ = operands[-1].shape
    pairs, tiles = steps.shape[0], 2
    shape = (pairs, stations, stations * tiles * 2, LANES)

    def body(*refs):
        out_ref, buf, sems = refs[len(operands) :]
        steps_ref, mine_ref, theirs_ref, *turned_ref = refs[0 if done is None else 1 : len(operands)]
        first = near_tile()
        column = lax.broadcasted_iota(jnp.int32, (stations, LANES), 0)

        def put(p, a, tile, value):
            for part in range(2):
                rows = value[part * stations : (part + 1) * stations]
                buf[p, a, pl.ds(tile * 2 + part, stations, stride=2 * tiles), :] = rows

        def hermitian(p, a, tile, above, below, middle):
            re = jnp.where(column > a, above[:stations], below[:stations])
            im = jnp.where(column > a, above[stations:], below[stations:])
            re = jnp.where(column == a, middle, re)
            im = jnp.where(column == a, jnp.zeros_like(im), im)
            put(p, a, tile, jnp.concatenate([re, im], axis=0))

        def store(p, part):
            rows = pl.ds(part * stations // 2, stations // 2)
            return pltpu.make_async_copy(buf.at[p, rows], out_ref.at[p, rows], sems.at[p, part])

        def fill(p, one):
            for part in range(2):
                for a in range(part * stations // 2, (part + 1) * stations // 2):
                    one(p, a)
                store(p, part).start()

        def edge(mine_tile):
            def one(p, a):
                put(p, a, mine_tile, mine_ref[a])
                put(p, a, 1 - mine_tile, theirs_ref[a].astype(WIDE))

            return one

        def itself(p, a):
            own, back = mine_ref[a], turned_ref[0][a].astype(WIDE)
            hermitian(p, a, 1 - first, own, back, own[:stations])
            hermitian(p, a, first, back, own, own[stations:])

        written = []
        for p in range(pairs):
            away = jnp.max(steps_ref[p])
            alone = jnp.abs(away) < 0.5
            inside = jnp.logical_and((away > 0.5) == (first == 1), jnp.logical_not(alone))
            if done is None:
                pl.when(inside)(lambda p=p: fill(p, edge(first)))
                written.append(inside)
            else:
                outside = jnp.logical_not(jnp.logical_or(alone, inside))
                pl.when(outside)(lambda p=p: fill(p, edge(1 - first)))
                pl.when(alone)(lambda p=p: fill(p, itself))
                written.append(jnp.logical_not(inside))
        for p in range(pairs):

            @pl.when(written[p])
            def _(p=p):
                for part in range(2):
                    store(p, part).wait()

    hbm = pl.BlockSpec(memory_space=pltpu.HBM)
    specs = [VMEM] * len(operands)
    if done is not None:
        specs[0] = hbm
    return pl.pallas_call(
        body,
        in_specs=specs,
        out_specs=hbm,
        out_shape=jax.ShapeDtypeStruct(shape, WIDE),
        scratch_shapes=[pltpu.VMEM(shape, WIDE), pltpu.SemaphoreType.DMA((pairs, 2))],
        input_output_aliases={} if done is None else {0: 0},
        compiler_params=limits(4),
        name="assemble",
    )(*operands)


def per_device(spectra, band_weight, station_order, pair_blocks):
    stations, _, windows, _, bins = spectra.shape
    tiles, pairs = bins // LANES, pair_blocks.shape[0]
    count, hours = lax.axis_size("sta"), lax.axis_size("hour")
    rows = spectra.reshape(stations, windows, 2, tiles, LANES)
    rows = rows.transpose(0, 1, 3, 2, 4).reshape(stations, windows, 2 * tiles, LANES)
    near, far, steps = whiten(rows, band_weight.reshape(tiles, LANES), station_order, pair_blocks, hours)

    on_chip = [(g, g ^ 1) for g in range(count)]
    across = [(g, h) for i in range(1, count - 1, 2) for g, h in ((i, i + 1), (i + 1, i))]

    def to_owner(part, d):
        return lax.ppermute(part, "hour", [(h, h ^ d) for h in range(hours)]) if d else part

    def after(value, *earlier):
        return lax.optimization_barrier((value, earlier))[0]

    near_others = lax.ppermute(far, "sta", on_chip)
    far_others = [lax.ppermute(near[0], "sta", across)]
    dtypes = [jnp.bfloat16 if d else WIDE for d in ORDER]
    scale = 1.0 / (hours * windows)

    near_made = [
        near_product(near[k // BATCH], k % BATCH, near_others, k, windows, dtypes[k])
        for k in range(hours)
    ]
    far_others.append(lax.ppermute(after(near[1], *near_made[:1]), "sta", across))
    near_parts = [to_owner(part, d) for part, d in zip(near_made, ORDER)]
    far_others[0] = after(far_others[0], *near_made)
    far_made = []
    for k in range(hours):
        batch, place = divmod(k, BATCH)
        if place == 0 and k:
            far_others[batch] = after(far_others[batch], *far_made)
        if k == 1:
            far_others[batch] = after(far_others[batch], near_parts[0], far_made[0])
        far_made.append(far_product(far, k, far_others[batch], near[batch], place, windows, dtypes[k]))
    far_parts = [to_owner(part, d) for part, d in zip(far_made, ORDER)]
    near_mine, turned = add_hours(after(near_parts[::-1], *far_made), scale)
    near_theirs = lax.ppermute(turned, "sta", on_chip)
    far_mine, turned = add_hours(after(far_parts[::-1], near_mine), scale)
    far_theirs = lax.ppermute(turned, "sta", across)
    cross = assemble(steps, (near_mine, near_theirs))
    cross = assemble(steps, None, (far_mine, far_theirs), turned, cross)
    cross = cross.reshape(pairs, stations, stations, tiles // hours, 2, LANES)
    return cross.transpose(0, 1, 2, 4, 3, 5).reshape(pairs, stations, stations, 2, bins // hours)


def solution(mesh):
    return jax.shard_map(
        per_device,
        mesh=mesh,
        in_specs=(P("sta", "hour", None, None, None), P(), P("sta", None), P("sta", None)),
        out_specs=P("sta", None, None, None, "hour"),
        check_vma=False,
    )
```
